32 devices in a mesh: groups: 2 (over y), area: 8 (over z, x), unit: 2 (over core).
Axes of the slice: x: 2, y: 2, z: 4, core: 2. Of those that a mesh axis runs over, the one named last changes fastest.
Arguments:
- state_start: float32 [64, 65536], P(None, ('groups', 'area', 'unit')), parts along dimension 1, may hold values from -6 to 6
- history: bfloat16 [6, 64, 12288], P(None, None, ('groups', 'area', 'unit')), parts along dimension 2, may hold values from -0.8984375 to 0.8984375
- external: float32 [64, 65536], P(None, ('groups', 'area', 'unit')), parts along dimension 1, may hold values from -4 to 4
- leak: float32 [65536], P(('groups', 'area', 'unit')), parts along dimension 0, may hold values from 0.05 to 0.6
- w_rec: bfloat16 [4096, 65536], P(None, ('groups', 'area', 'unit')), parts along dimension 1, may hold values from -0.09375 to 0.09375
- w_in: bfloat16 [768, 65536], P(None, ('groups', 'area', 'unit')), parts along dimension 1, may hold values from -0.21875 to 0.21875
- sources: int32 [16, 6], P('groups'), parts along dimension 0, may hold values from -1 to 7, as said below
- delays: int32 [16, 6], P('groups'), parts along dimension 0, may hold values from 3 to 6
- gains: float32 [16, 6], P('groups'), parts along dimension 0, may hold values from 0.3 to 1.5
- proj_units: int32 [12288], P(('groups', 'area', 'unit')), parts along dimension 0, may hold values from 0 to 4095, as said below
Outputs:
- state_end: float32 [64, 65536], P(None, ('groups', 'area', 'unit')), parts along dimension 1
- produced: bfloat16 [6, 64, 12288], P(None, None, ('groups', 'area', 'unit')), parts along dimension 2
The draws below stay inside these ranges and needn't reach their ends.
There are 2 independent parts, one for each index of `groups`. The reference program is written for one: setup_inputs(seed, part) draws one part's arguments, and reference() takes and returns one part's arrays. A program takes and returns all parts, laid end to end along the dimension named above; each array names one. Nothing has to cross between parts.
Inputs may be any that keep to these rules, and one draw needn't show every extreme that they name: Row a names, in its first 2 to 6 entries, distinct source areas other than a; its other entries are -1. Some row has 6 sources and some row 2, at rows drawn from the seed. `proj_units`: the 768 entries of one area are distinct units of that area.
All inputs are finite; a program needn't handle non-finite values.
Results may differ from the reference program's by a relative error of at most 0.0023.
Values may be sent and summed in bfloat16 or wider, within the bound.
No kernel may reach another device: no remote copies, remote signals or barrier semaphores. Data moves between devices by JAX's collectives and lax.ppermute only.
A program may use at most 64 MiB of HBM per device.

```python
import math
from functools import partial
import jax
import jax.numpy as jnp
from jax import lax

UNITS = 4096
PROJ = 768
TRIALS = 64
MAXSRC = 6
WIN = 3
WINDOWS = 2
AREAS = 8


def draw_sources(key, part):
    row_keys = jax.random.split(jax.random.fold_in(key, 11), AREAS)

    def offsets_row(row_key):
        return jax.random.permutation(row_key, AREAS - 1)[:MAXSRC] + 1
    offsets = jax.vmap(offsets_row)(row_keys)
    target_ids = jnp.arange(AREAS, dtype=jnp.int32)[:, None]
    picked = (target_ids + offsets) % AREAS
    counts = jax.random.randint(jax.random.fold_in(key, 12), (AREAS,), 2, MAXSRC + 1)
    first_row = jax.random.randint(jax.random.fold_in(key, 13), (), 0, AREAS)
    second_row = (first_row + 1 + jax.random.randint(jax.random.fold_in(key, 14), (), 0, AREAS - 1)) % AREAS
    counts = counts.at[first_row].set(MAXSRC).at[second_row].set(2)
    slot_ids = jnp.arange(MAXSRC, dtype=jnp.int32)[None, :]
    return jnp.where(slot_ids < counts[:, None], picked, -1).astype(jnp.int32)


def draw_proj_units(key, part):
    area_keys = jax.random.split(jax.random.fold_in(key, 21), AREAS)

    def one_area(area_key):
        return jax.random.permutation(area_key, UNITS)[:PROJ]
    return jax.vmap(one_area)(area_keys).reshape(-1).astype(jnp.int32)


def set_ends(array, rng, least, largest):
    dims = array.shape
    spot = [jax.random.randint(jax.random.fold_in(rng, axis), (), 0, dims[axis]) for axis in range(len(dims))]
    array = array.at[tuple(spot)].set(least)
    longest = dims.index(max(dims))
    spot[longest] = (spot[longest] + 1) % dims[longest]
    return array.at[tuple(spot)].set(largest)


def block_scale(own_key, shape, cuts, low, largest):
    def one(position, shards_of):
        heights = jax.random.uniform(jax.random.fold_in(jax.random.fold_in(own_key, 6), position), (shards_of,), jnp.float32, low / len(cuts), largest / len(cuts))
        return jnp.repeat(jnp.exp(heights), shape[position] // shards_of).reshape((-1,) + (1,) * (len(shape) - position - 1))

    level = one(*cuts[0])
    for cut in cuts[1:]:
        level = level * one(*cut)
    return level


def gaussian(own_key, shape, deviation, reach, shards=(), kind=jnp.bfloat16):
    entries = jax.random.normal(own_key, shape, jnp.float32) * deviation
    if len(shards) > 0:
        entries = block_scale(own_key, shape, shards, -0.22, 0.18) * entries
    return jnp.clip(entries, min=-reach, max=reach).astype(kind)


def setup_inputs(seed: int = 0, part: int = 0) -> dict:
    key_list = jax.random.split(jax.random.key(seed), 11)
    own_keys = jax.random.split(jax.random.fold_in(key_list[10], part), 11)
    return {
        "state_start": gaussian(own_keys[0], (TRIALS, AREAS * UNITS), 1.0, 6.0, ((1, 16),), jnp.float32),
        "history": jnp.clip(jax.random.uniform(own_keys[1], (2 * WIN, TRIALS, AREAS * PROJ), jnp.float32, -0.8984375, 0.8984375) * block_scale(own_keys[1], (2 * WIN, TRIALS, AREAS * PROJ), ((2, 16),), -0.4, 0.0), -0.8984375, 0.8984375).astype(jnp.bfloat16),
        "external": gaussian(own_keys[2], (TRIALS, AREAS * UNITS), 0.5, 4.0, ((1, 16),), jnp.float32),
        "leak": jnp.clip(jnp.exp(math.log(0.6) - 2.4849067 * jax.random.uniform(own_keys[3], (AREAS * UNITS,), jnp.float32) ** block_scale(own_keys[3], (AREAS * UNITS,), ((0, 16),), -0.2, 0.2)), 0.05, 0.6),
        "w_rec": gaussian(own_keys[4], (UNITS, AREAS * UNITS), UNITS ** -0.5, 0.09375, ((1, 16),)),
        "w_in": gaussian(own_keys[5], (PROJ, AREAS * UNITS), PROJ ** -0.5, 0.21875, ((1, 16),)),
        "sources": draw_sources(jax.random.fold_in(jax.random.fold_in(key_list[10], part), 71), part),
        "delays": set_ends(jax.random.randint(own_keys[7], (AREAS, MAXSRC), WIN, 2 * WIN + 1), jax.random.fold_in(own_keys[7], 1), WIN, 2 * WIN).astype(jnp.int32),
        "gains": jnp.clip(jnp.exp(jax.random.uniform(own_keys[8], (AREAS, MAXSRC), jnp.float32, math.log(0.3), math.log(1.5))), 0.3, 1.5),
        "proj_units": draw_proj_units(jax.random.fold_in(jax.random.fold_in(key_list[10], part), 71), part),
    }


def drive_one(known, first_time, row_args):
    row_src, row_delay, row_gain = row_args
    valid = row_src >= 0
    picked = known[jnp.maximum(row_src, 0)].astype(jnp.float32)
    span_len = known.shape[1]
    times = first_time + jnp.arange(WIN, dtype=jnp.int32)
    target_idx = times[:, None] - row_delay[None, :] + 2 * WIN
    columns = jnp.arange(span_len, dtype=jnp.int32)
    select = (columns[None, None, :] == target_idx[:, :, None]) & valid[None, :, None]
    weight = jnp.where(select, row_gain[None, :, None], jnp.float32(0.0))
    summed = jnp.einsum("ikj,kjbp->ibp", weight, picked, precision=lax.Precision.HIGHEST)
    return summed.astype(jnp.bfloat16)


def area_window(w_rec, w_in, area_args):
    state_now, area_id, leak_row, drive_win, ext_row, proj_row = area_args
    weight_rec = lax.dynamic_slice_in_dim(w_rec, area_id * UNITS, UNITS, 1)
    weight_in = lax.dynamic_slice_in_dim(w_in, area_id * UNITS, UNITS, 1)
    current = jnp.dot(drive_win.reshape(WIN * TRIALS, PROJ), weight_in, preferred_element_type=jnp.float32)
    current = current.reshape(WIN, TRIALS, UNITS)
    fresh = []
    for inner_step in range(WIN):
        rate_rows = jnp.tanh(state_now).astype(jnp.bfloat16)
        recur = jnp.dot(rate_rows, weight_rec, preferred_element_type=jnp.float32)
        fresh.append(rate_rows[:, proj_row])
        state_now = state_now + leak_row[None, :] * (-state_now + recur + current[inner_step] + ext_row)
    return state_now, jnp.stack(fresh)


def reference(state_start, history, external, leak, w_rec, w_in, sources, delays, gains, proj_units):
    known = jnp.transpose(history.reshape(2 * WIN, TRIALS, AREAS, PROJ), (2, 0, 1, 3))
    state_now = jnp.transpose(state_start.reshape(TRIALS, AREAS, UNITS), (1, 0, 2))
    ext_all = jnp.transpose(external.reshape(TRIALS, AREAS, UNITS), (1, 0, 2))
    leak_rows = leak.reshape(AREAS, UNITS)
    proj_rows = proj_units.reshape(AREAS, PROJ)
    area_ids = jnp.arange(AREAS, dtype=jnp.int32)
    produced = []
    for window_idx in range(WINDOWS):
        drive_all = lax.map(partial(drive_one, known, window_idx * WIN), (sources, delays, gains))
        state_now, fresh = lax.map(partial(area_window, w_rec, w_in), (state_now, area_ids, leak_rows, drive_all, ext_all, proj_rows))
        known = jnp.concatenate([known, fresh], axis=1)
        produced.append(fresh)
    produced_all = jnp.concatenate(produced, axis=1)
    produced_all = jnp.transpose(produced_all, (1, 2, 0, 3)).reshape(WINDOWS * WIN, TRIALS, AREAS * PROJ)
    state_end = jnp.transpose(state_now, (1, 0, 2)).reshape(TRIALS, AREAS * UNITS)
    return state_end, produced_all
```

```python
import functools

import jax
import jax.numpy as jnp
from jax import lax
from jax.experimental import pallas as pl
from jax.experimental.pallas import tpu as pltpu
from jax.sharding import PartitionSpec as P

MAXSRC = 6
WIN = 3
WINDOWS = 2
STEPS = WIN * WINDOWS
BF16 = jnp.bfloat16
F32 = jnp.float32
VM = pl.BlockSpec(memory_space=pltpu.VMEM)
SM = pl.BlockSpec(memory_space=pltpu.SMEM)
MIB = 1 << 20


def swapped(value, axis, stride):
    mask = 2**stride
    return crossed(value, axis, mask)


def crossed(value, axis, mask):
    pairs = [(source, source ^ mask) for source in range(lax.axis_size(axis))]
    return lax.ppermute(value, axis, pairs)


def shaped(shape, kind):
    return jax.ShapeDtypeStruct(shape, kind)


def params(limit=8):
    return pltpu.CompilerParams(vmem_limit_bytes=limit * MIB)


def onehot_kernel(units_ref, out_ref):
    rows, cols = out_ref.shape
    block = 256
    units = units_ref[...]
    for start in range(0, rows, block):
        ids = lax.broadcasted_iota(jnp.int32, (block, cols), 0) + start
        out_ref[start : start + block, :] = jnp.where(ids == units, 1.0, 0.0).astype(BF16)


def onehot(units, rows):
    cols = units.shape[0]
    return pl.pallas_call(
        onehot_kernel,
        out_shape=shaped((rows, cols), BF16),
        in_specs=[VM],
        out_specs=VM,
        compiler_params=params(),
        name="onehot",
    )(units.reshape(1, cols))


def half_rows(unit, ref, block):
    count = block.shape[1]
    return pl.ds(pl.multiple_of(unit * count, count), count)


def pick_kernel(place_ref, own_ref, other_ref, select_ref, out_ref):
    unit = place_ref[1]
    picked = jnp.dot(
        own_ref[...], select_ref[half_rows(unit, select_ref, own_ref), :], preferred_element_type=F32
    )
    picked += jnp.dot(
        other_ref[...],
        select_ref[half_rows(1 - unit, select_ref, other_ref), :],
        preferred_element_type=F32,
    )
    out_ref[...] = picked.astype(BF16)


def pick(place, own, other, select):
    return pl.pallas_call(
        pick_kernel,
        out_shape=shaped((own.shape[0], select.shape[1]), BF16),
        in_specs=[SM, VM, VM, VM],
        out_specs=VM,
        compiler_params=params(),
        name="pick",
    )(place, own, other, select)


def columns_of(width):
    step = 256 if width % 256 == 0 else width
    return [slice(start, start + step) for start in range(0, width, step)]


def own_kernel(place_ref, rates_ref, weight_ref, extra_ref, out_ref):
    rows = half_rows(place_ref[1], weight_ref, rates_ref)
    for cols in columns_of(out_ref.shape[1]):
        out_ref[:, cols] = extra_ref[:, cols] + jnp.dot(
            rates_ref[...], weight_ref[rows, cols], preferred_element_type=F32
        )


def own_part(place, rates, weight, extra):
    return pl.pallas_call(
        own_kernel,
        out_shape=shaped(extra.shape, F32),
        in_specs=[SM, VM, VM, VM],
        out_specs=VM,
        compiler_params=params(),
        name="own_part",
    )(place, rates, weight, extra)


def other_kernel(place_ref, rates_ref, weight_ref, extra_ref, out_ref):
    rows = half_rows(1 - place_ref[1], weight_ref, rates_ref)
    for cols in columns_of(out_ref.shape[1]):
        out_ref[:, cols] = extra_ref[:, cols] + jnp.dot(
            rates_ref[...], weight_ref[rows, cols], preferred_element_type=F32
        )


def other_part(place, rates, weight, extra):
    return pl.pallas_call(
        other_kernel,
        out_shape=shaped(extra.shape, F32),
        in_specs=[SM, VM, VM, VM],
        out_specs=VM,
        compiler_params=params(),
        name="other_part",
    )(place, rates, weight, extra)


def first_kernel(place_ref, own_ref, other_ref, weight_ref, sum_ref, state_ref, leak_ref, new_ref, rates_ref):
    unit = place_ref[1]
    own_rows = half_rows(unit, weight_ref, own_ref)
    other_rows = half_rows(1 - unit, weight_ref, other_ref)
    for cols in columns_of(new_ref.shape[1]):
        total = sum_ref[:, cols]
        total += jnp.dot(own_ref[...], weight_ref[own_rows, cols], preferred_element_type=F32)
        total += jnp.dot(other_ref[...], weight_ref[other_rows, cols], preferred_element_type=F32)
        state = state_ref[:, cols]
        state = state + leak_ref[:, cols] * (total - state)
        new_ref[:, cols] = state
        rates_ref[:, cols] = jnp.tanh(state).astype(BF16)


def first_step(place, own, other, weight, total, state, leak):
    return pl.pallas_call(
        first_kernel,
        out_shape=(shaped(state.shape, F32), shaped(state.shape, BF16)),
        in_specs=[SM] + [VM] * 6,
        out_specs=(VM, VM),
        compiler_params=params(),
        name="first_step",
    )(place, own, other, weight, total, state, leak)


def step_kernel(row, last, place_ref, rates_ref, weight_ref, sum_ref, cur_ref, state_ref, leak_ref, new_ref, *outs):
    rows = half_rows(1 - place_ref[1], weight_ref, rates_ref)
    trials = new_ref.shape[0]
    for cols in columns_of(new_ref.shape[1]):
        total = sum_ref[:, cols] + cur_ref[row * trials : (row + 1) * trials, cols]
        total += jnp.dot(rates_ref[...], weight_ref[rows, cols], preferred_element_type=F32)
        state = state_ref[:, cols]
        state = state + leak_ref[:, cols] * (total - state)
        new_ref[:, cols] = state
        if not last:
            outs[0][:, cols] = jnp.tanh(state).astype(BF16)


def step(place, rates, weight, total, current, row, state, leak, last):
    outs = [shaped(state.shape, F32)] + ([] if last else [shaped(state.shape, BF16)])
    return pl.pallas_call(
        functools.partial(step_kernel, row, last),
        out_shape=tuple(outs),
        in_specs=[SM] + [VM] * 6,
        out_specs=(VM,) * len(outs),
        compiler_params=params(),
        name="step",
    )(place, rates, weight, total, current, state, leak)


def current_kernel(place_ref, own_ref, other_ref, weight_ref, out_ref):
    unit = place_ref[1]
    own_rows = half_rows(unit, weight_ref, own_ref)
    other_rows = half_rows(1 - unit, weight_ref, other_ref)
    for cols in columns_of(out_ref.shape[1]):
        total = jnp.dot(own_ref[...], weight_ref[own_rows, cols], preferred_element_type=F32)
        total += jnp.dot(other_ref[...], weight_ref[other_rows, cols], preferred_element_type=F32)
        out_ref[:, cols] = total


def current_of(place, own, other, weight):
    return pl.pallas_call(
        current_kernel,
        out_shape=shaped((own.shape[0], weight.shape[1]), F32),
        in_specs=[SM, VM, VM, VM],
        out_specs=VM,
        compiler_params=params(),
        name="current",
    )(place, own, other, weight)


def partial_kernel(times, count, slots, place_ref, src_ref, delay_ref, gain_ref, *refs):
    fields, outs = refs[:-count], refs[-count:]
    area = place_ref[0]
    spans = {}
    for ref, (who, first) in zip(fields, slots):
        for pos in range(ref.shape[0]):
            spans[who, first + pos] = (ref, pos)
    for line in range(count):
        target = area ^ (2 * line)
        found = []
        for who in range(2):
            source = area ^ who
            delay, gain = jnp.int32(0), jnp.float32(0.0)
            for slot in range(MAXSRC):
                match = src_ref[target, slot] == source
                delay += jnp.where(match, delay_ref[target, slot], 0)
                gain += jnp.where(match, gain_ref[target, slot], 0.0)
            found.append([jnp.where(delay == lag, gain, 0.0) for lag in range(WIN, 2 * WIN + 1)])
        for index, time in enumerate(times):
            total = None
            for who in range(2):
                for lag in range(WIN, 2 * WIN + 1):
                    ref, pos = spans[who, time - lag]
                    term = found[who][lag - WIN] * ref[pos].astype(F32)
                    total = term if total is None else total + term
            outs[line][index] = total.astype(outs[line].dtype)


def partials(place, tables, times, count, fields):
    trials, part = fields[0][2].shape[1:]
    span = len(times)
    outs = [shaped((span, trials, part), F32)] + [shaped((span, trials, part), BF16)] * (count - 1)
    return pl.pallas_call(
        functools.partial(partial_kernel, times, count, [field[:2] for field in fields]),
        out_shape=tuple(outs),
        in_specs=[SM] * 4 + [VM] * len(fields),
        out_specs=(VM,) * count,
        compiler_params=params(),
        name="partials",
    )(place, *tables, *[field[2] for field in fields])


def drive_kernel(own_ref, *refs):
    total = own_ref[...]
    for ref in refs[:-1]:
        total += ref[...].astype(F32)
    refs[-1][...] = total.astype(BF16).reshape(refs[-1].shape)


def drive_of(own, arrived):
    span, trials, part = own.shape
    return pl.pallas_call(
        drive_kernel,
        out_shape=shaped((span * trials, part), BF16),
        in_specs=[VM] * (1 + len(arrived)),
        out_specs=VM,
        compiler_params=params(),
        name="drive",
    )(own, *arrived)


def body(state_start, history, external, leak, w_rec, w_in, sources, delays, gains, proj_units):
    area = lax.axis_index("area").astype(jnp.int32)
    unit = lax.axis_index("unit").astype(jnp.int32)
    place = jnp.stack([area, unit])
    tables = (sources, delays, gains)
    line_count = lax.axis_size("area") // 2
    leak_row = leak.reshape(1, -1)
    known = [(0, -2 * WIN, history), (1, -2 * WIN, crossed(history, "area", 1))]

    rates = jnp.tanh(state_start).astype(BF16)
    other = crossed(rates, "unit", 1)
    total = own_part(place, rates, w_rec, external)
    select = onehot(proj_units, w_rec.shape[0])
    picks = [pick(place, rates, other, select)]
    total = other_part(place, other, w_rec, total)

    def share_pick(time):
        value = picks[time][None]
        return [(0, time, value), (1, time, crossed(value, "area", 1))]

    def send(times, fields):
        sums = partials(place, tables, times, line_count, fields)
        arrived = [crossed(sums[line], "area", 2 * line) for line in range(1, line_count)]
        return sums[0], arrived

    def drive_pair(sent):
        own = drive_of(*sent)
        return own, crossed(own, "unit", 1)

    sent_first = send((0,), known)
    known += share_pick(0)
    sent_next = send(tuple(range(1, WIN + 1)), known)
    state, rates = first_step(place, *drive_pair(sent_first), w_in, total, state_start, leak_row)

    current = None
    sent_late = []
    for time in range(1, STEPS):
        other = crossed(rates, "unit", 1)
        total = own_part(place, rates, w_rec, external)
        picks.append(pick(place, rates, other, select))
        if time < WIN:
            known += share_pick(time)
            sent_late.append(send((time + WIN,), known))
        if time == 1:
            current = current_of(place, *drive_pair(sent_next), w_in)
        if time > WIN:
            current = current_of(place, *drive_pair(sent_late[time - WIN - 1]), w_in)
        row = time - 1 if time <= WIN else 0
        last = time == STEPS - 1
        new = step(place, other, w_rec, total, current, row, state, leak_row, last)
        state = new[0]
        if not last:
            rates = new[1]
    return state, jnp.stack(picks)


def wide_body(state_start, history, external, leak, w_rec, w_in, sources, delays, gains, proj_units):
    area_count = lax.axis_size("area")
    area_index = lax.axis_index("area")
    area_total = sources.shape[0]
    share = area_count // area_total
    own_area = area_index // share
    own_src = lax.dynamic_slice_in_dim(sources, own_area, 1, 0)[0]
    own_delay = lax.dynamic_slice_in_dim(delays, own_area, 1, 0)[0]
    own_gain = lax.dynamic_slice_in_dim(gains, own_area, 1, 0)[0]
    own_valid = own_src >= 0
    trial_count = state_start.shape[0]
    proj_part = proj_units.shape[0]
    unit_full = w_rec.shape[0]
    proj_full = w_in.shape[0]
    bit_count = share.bit_length() - 1
    select = (jnp.arange(unit_full, dtype=jnp.int32)[:, None] == proj_units[None, :]).astype(BF16)
    state_now = state_start
    received = []
    outgoing = history
    produced = []
    for window_idx in range(WINDOWS):
        move_span_len = outgoing.shape[0]
        flat = outgoing.reshape(1, -1)
        wanted = (own_src[:, None] * share + jnp.arange(share, dtype=jnp.int32)[None, :]).reshape(-1)
        piece = lax.all_gather(flat, "area", axis=0, tiled=True)
        count = piece.shape[0]
        match = wanted[:, None] == jnp.arange(count, dtype=jnp.int32)[None, :]
        total = jnp.dot(match.astype(BF16), piece, preferred_element_type=F32)
        received.append(
            total.astype(BF16).reshape(MAXSRC, share, move_span_len, trial_count, proj_part)
        )
        known = jnp.concatenate(received, axis=2)
        span_len = known.shape[2]
        times = window_idx * WIN + jnp.arange(WIN, dtype=jnp.int32)
        target_idx = times[:, None] - own_delay[None, :] + 2 * WIN
        columns = jnp.arange(span_len, dtype=jnp.int32)
        chosen_steps = (columns[None, None, :] == target_idx[:, :, None]) & own_valid[None, :, None]
        weight = jnp.where(chosen_steps, own_gain[None, :, None], jnp.float32(0.0))
        summed = jnp.einsum(
            "ikj,kqjbp->ibqp", weight, known.astype(F32), precision=lax.Precision.HIGHEST
        )
        drive_part = summed.astype(BF16)
        drive_full = lax.all_gather(drive_part[:, :, :, None, :], "unit", axis=3, tiled=True)
        current = jnp.dot(
            drive_full.reshape(WIN * trial_count, proj_full), w_in, preferred_element_type=F32
        )
        current = current.reshape(WIN, trial_count, -1)
        fresh = []
        for inner_step in range(WIN):
            rate_rows = jnp.tanh(state_now).astype(BF16)
            joined = lax.all_gather(rate_rows, "unit", axis=1, tiled=True)
            for bit in range(bit_count):
                other = swapped(joined, "area", bit)
                upper = area_index // (1 << bit) % 2 == 1
                joined = jnp.where(
                    upper,
                    jnp.concatenate([other, joined], axis=1),
                    jnp.concatenate([joined, other], axis=1),
                )
            recur = jnp.dot(joined, w_rec, preferred_element_type=F32)
            picked = jnp.dot(joined, select, preferred_element_type=F32)
            fresh.append(picked.astype(BF16))
            state_now = state_now + leak[None, :] * (
                -state_now + recur + current[inner_step] + external
            )
        outgoing = jnp.stack(fresh)
        produced.append(outgoing)
    return (state_now, jnp.concatenate(produced, axis=0))


def solution(mesh):
    split = P(None, ("groups", "area", "unit"))
    placed = (
        split,
        P(None, None, ("groups", "area", "unit")),
        split,
        P(("groups", "area", "unit")),
        split,
        split,
        P("groups", None),
        P("groups", None),
        P("groups", None),
        P(("groups", "area", "unit")),
    )

    def chosen(*args):
        areas = lax.axis_size("area")
        narrow = args[6].shape[0] == areas and lax.axis_size("unit") == 2 and areas & (areas - 1) == 0
        return (body if narrow else wide_body)(*args)

    return jax.shard_map(
        chosen,
        mesh=mesh,
        in_specs=placed,
        out_specs=(split, P(None, None, ("groups", "area", "unit"))),
        check_vma=False,
    )
```

```python
import functools

import jax
import jax.numpy as jnp
from jax import lax
from jax.experimental import pallas as pl
from jax.experimental.pallas import tpu as pltpu
from jax.sharding import PartitionSpec as P

MAXSRC = 6
WIN = 3
WINDOWS = 2
STEPS = WIN * WINDOWS
BF16 = jnp.bfloat16
F32 = jnp.float32
VM = pl.BlockSpec(memory_space=pltpu.VMEM)
SM = pl.BlockSpec(memory_space=pltpu.SMEM)
HB = pl.BlockSpec(memory_space=pltpu.MemorySpace.HBM)
LAGS = range(WIN, 2 * WIN + 1)
MIB = 1 << 20
CODE = 8192.0


def swapped(value, axis, stride):
    mask = 2**stride
    return crossed(value, axis, mask)


def crossed(value, axis, mask):
    pairs = [(source, source ^ mask) for source in range(lax.axis_size(axis))]
    return lax.ppermute(value, axis, pairs)


def shaped(shape, kind):
    return jax.ShapeDtypeStruct(shape, kind)


def params(limit=8):
    return pltpu.CompilerParams(vmem_limit_bytes=limit * MIB)


def half_rows(unit, block):
    count = block.shape[1]
    return pl.ds(pl.multiple_of(unit * count, count), count)


def columns_of(width):
    size = 256 if width % 256 == 0 else width
    return [slice(start, start + size) for start in range(0, width, size)]


def matmul(left, right):
    return jnp.dot(left, right, preferred_element_type=F32)


def stage_kernel(lines, copies, area_ref, unit_ref, src_ref, delay_ref, gain_ref, units_ref, *refs):
    held, refs = refs[:copies], refs[copies:]
    outs, (select_ref, coef_ref, sems) = refs[:copies], refs[copies:]
    moves = []
    for index, (source, target) in enumerate(zip(held, outs)):
        moves.append(pltpu.make_async_copy(source, target, sems.at[index]))
        moves[-1].start()
    area = area_ref[0]
    width = coef_ref.shape[1]
    row = 0
    for line in range(lines):
        target = area ^ (2 * line)
        for who in range(2):
            source = area ^ who
            delay, gain = jnp.int32(0), jnp.float32(0.0)
            for slot in range(MAXSRC):
                match = src_ref[target, slot] == source
                delay += jnp.where(match, delay_ref[target, slot], 0)
                gain += jnp.where(match, gain_ref[target, slot], 0.0)
            for lag in LAGS:
                value = jnp.where(delay == lag, gain, 0.0)
                coef_ref[row : row + 1, :] = jnp.full((1, width), value, F32)
                row += 1
    rows, cols = select_ref.shape
    block = 256
    units = units_ref[...]
    for start in range(0, rows, block):
        ids = lax.broadcasted_iota(jnp.int32, (block, cols), 0) + start
        select_ref[start : start + block, :] = jnp.where(ids == units, 1.0, 0.0).astype(BF16)
    for move in moves:
        move.wait()


def held_far(array):
    return pltpu.with_memory_space_constraint(array, pltpu.MemorySpace.HBM)


def stage(area, unit, tables, units, lines, arrays):
    cols = units.shape[0]
    rows = arrays[0].shape[0]
    outs = [pltpu.VMEM(array.shape, array.dtype) for array in arrays]
    outs.append(pltpu.VMEM((rows, cols), BF16))
    outs.append(pltpu.VMEM((lines * 2 * len(LAGS), cols), F32))
    return pl.pallas_call(
        functools.partial(stage_kernel, lines, len(arrays)),
        out_shape=tuple(outs),
        in_specs=[SM] * 5 + [VM] + [HB] * len(arrays),
        out_specs=(VM,) * len(outs),
        scratch_shapes=[pltpu.SemaphoreType.DMA((len(arrays),))],
        compiler_params=params(),
        name="stage",
    )(area, unit, *tables, units.reshape(1, cols), *[held_far(array) for array in arrays])


def pick_kernel(unit_ref, own_ref, other_ref, select_ref, out_ref):
    unit = unit_ref[0]
    picked = matmul(own_ref[...], select_ref[half_rows(unit, own_ref), :])
    picked += matmul(other_ref[...], select_ref[half_rows(1 - unit, other_ref), :])
    out_ref[...] = picked.astype(BF16)


def pick(unit, own, other, select):
    return pl.pallas_call(
        pick_kernel,
        out_shape=shaped((own.shape[0], select.shape[1]), BF16),
        in_specs=[SM, VM, VM, VM],
        out_specs=VM,
        compiler_params=params(),
        name="pick",
    )(unit, own, other, select)


def opening_kernel(unit_ref, own_ref, other_ref, weight_ref, extra_ref, select_ref, out_ref, pick_ref):
    unit = unit_ref[0]
    own_rows, other_rows = half_rows(unit, own_ref), half_rows(1 - unit, other_ref)
    for cols in columns_of(out_ref.shape[1]):
        total = extra_ref[:, cols] + matmul(own_ref[...], weight_ref[own_rows, cols])
        out_ref[:, cols] = total + matmul(other_ref[...], weight_ref[other_rows, cols])
    picked = matmul(own_ref[...], select_ref[own_rows, :])
    picked += matmul(other_ref[...], select_ref[other_rows, :])
    pick_ref[...] = picked.astype(BF16)


def opening(unit, own, other, weight, extra, select):
    return pl.pallas_call(
        opening_kernel,
        out_shape=(shaped(extra.shape, F32), shaped((own.shape[0], select.shape[1]), BF16)),
        in_specs=[SM] + [VM] * 5,
        out_specs=(VM, VM),
        compiler_params=params(),
        name="opening",
    )(unit, own, other, weight, extra, select)


def own_kernel(picks, unit_ref, rates_ref, weight_ref, extra_ref, select_ref, out_ref, *pick_ref):
    rows = half_rows(unit_ref[0], rates_ref)
    for cols in columns_of(out_ref.shape[1]):
        out_ref[:, cols] = extra_ref[:, cols] + matmul(rates_ref[...], weight_ref[rows, cols])
    if picks:
        pick_ref[0][...] = matmul(rates_ref[...], select_ref[rows, :])


def own_part(unit, rates, weight, extra, select, picks):
    outs = [shaped(extra.shape, F32)]
    if picks:
        outs.append(shaped((rates.shape[0], select.shape[1]), F32))
    return pl.pallas_call(
        functools.partial(own_kernel, picks),
        out_shape=tuple(outs),
        in_specs=[SM] + [VM] * 4,
        out_specs=(VM,) * len(outs),
        compiler_params=params(),
        name="own_part",
    )(unit, rates, weight, extra, select)


def renewed(cols, total, state_ref, leak_ref):
    state = state_ref[:, cols]
    return state + leak_ref[:, cols] * (total - state)


def driven(unit, row, trials, own_ref, other_ref, weight_ref, cols):
    own_rows, other_rows = half_rows(unit, own_ref), half_rows(1 - unit, other_ref)
    lines = slice(row * trials, (row + 1) * trials)
    total = matmul(own_ref[lines, :], weight_ref[own_rows, cols])
    return total + matmul(other_ref[lines, :], weight_ref[other_rows, cols])


def first_kernel(unit_ref, own_ref, other_ref, weight_ref, sum_ref, state_ref, leak_ref, new_ref, rates_ref):
    for cols in columns_of(new_ref.shape[1]):
        total = sum_ref[:, cols]
        total += driven(unit_ref[0], 0, total.shape[0], own_ref, other_ref, weight_ref, cols)
        state = renewed(cols, total, state_ref, leak_ref)
        new_ref[:, cols] = state
        rates_ref[:, cols] = jnp.tanh(state).astype(BF16)


def first_step(unit, drives, weight, total, state, leak):
    return pl.pallas_call(
        first_kernel,
        out_shape=(shaped(state.shape, F32), shaped(state.shape, BF16)),
        in_specs=[SM] + [VM] * 6,
        out_specs=(VM, VM),
        compiler_params=params(),
        name="first_step",
    )(unit, *drives, weight, total, state, leak)


def step_kernel(row, picks, unit_ref, rates_ref, weight_ref, sum_ref, own_ref, other_ref, in_ref, state_ref, leak_ref, *refs):
    unit = unit_ref[0]
    rows = half_rows(1 - unit, rates_ref)
    if picks:
        select_ref, half_ref, new_ref, next_ref, pick_ref = refs
        picked = half_ref[...] + matmul(rates_ref[...], select_ref[rows, :])
        pick_ref[...] = picked.astype(BF16)
    else:
        new_ref, next_ref = refs
    for cols in columns_of(new_ref.shape[1]):
        total = sum_ref[:, cols] + matmul(rates_ref[...], weight_ref[rows, cols])
        total += driven(unit, row, total.shape[0], own_ref, other_ref, in_ref, cols)
        state = renewed(cols, total, state_ref, leak_ref)
        new_ref[:, cols] = state
        next_ref[:, cols] = jnp.tanh(state).astype(BF16)


def step(unit, rates, weight, total, drives, row, w_in, state, leak, select, half):
    picks = half is not None
    outs = [shaped(state.shape, F32), shaped(state.shape, BF16)]
    if picks:
        outs.append(shaped(half.shape, BF16))
    more = (select, half) if picks else ()
    return pl.pallas_call(
        functools.partial(step_kernel, row, picks),
        out_shape=tuple(outs),
        in_specs=[SM] + [VM] * (8 + len(more)),
        out_specs=(VM,) * len(outs),
        compiler_params=params(),
        name="step",
    )(unit, rates, weight, total, *drives, w_in, state, leak, *more)


def last_kernel(
    row, unit_ref, rates_ref, weight_ref, sum_ref, own_ref, other_ref, in_ref, state_ref, leak_ref, select_ref, half_ref, *refs
):
    old_refs, (new_ref, all_ref, fresh, state_buf, sems) = refs[:-5], refs[-5:]
    unit = unit_ref[0]
    rows = half_rows(1 - unit, rates_ref)
    moves = []

    def send(source, target):
        moves.append(pltpu.make_async_copy(source, target, sems.at[len(moves)]))
        moves[-1].start()

    for index, old in enumerate(old_refs):
        send(old, all_ref.at[index])
    picked = half_ref[...] + matmul(rates_ref[...], select_ref[rows, :])
    fresh[...] = picked.astype(BF16)
    send(fresh, all_ref.at[len(old_refs)])
    for cols in columns_of(state_buf.shape[1]):
        total = sum_ref[:, cols] + matmul(rates_ref[...], weight_ref[rows, cols])
        total += driven(unit, row, total.shape[0], own_ref, other_ref, in_ref, cols)
        state_buf[:, cols] = renewed(cols, total, state_ref, leak_ref)
        send(state_buf.at[:, cols], new_ref.at[:, cols])
    for move in moves:
        move.wait()


def last_step(unit, rates, weight, total, drives, row, w_in, state, leak, select, half, old):
    count = len(old) + 1 + len(columns_of(state.shape[1]))
    return pl.pallas_call(
        functools.partial(last_kernel, row),
        out_shape=(shaped(state.shape, F32), shaped((len(old) + 1,) + half.shape, BF16)),
        in_specs=[SM] + [VM] * (10 + len(old)),
        out_specs=(HB, HB),
        scratch_shapes=[
            pltpu.VMEM(half.shape, BF16),
            pltpu.VMEM(state.shape, F32),
            pltpu.SemaphoreType.DMA((count,)),
        ],
        compiler_params=params(),
        name="last_step",
    )(unit, rates, weight, total, *drives, w_in, state, leak, select, half, *old)


def coded(value):
    return jnp.round(value * CODE).astype(jnp.int32).astype(jnp.int16)


def decoded(value):
    return value.astype(jnp.int32).astype(F32) * (1.0 / CODE)


def partial_kernel(groups, lines, slots, coef_ref, *refs):
    fields, outs = refs[: len(slots)], refs[len(slots) :]
    trials = fields[0].shape[-2]
    size = 16 if trials % 16 == 0 else trials
    spans = {}
    for ref, (who, first) in zip(fields, slots):
        for pos in range(ref.shape[0]):
            spans[who, first + pos] = (ref, pos)
    for start in range(0, trials, size):
        band = slice(start, start + size)
        for number, times in enumerate(groups):
            for index, time in enumerate(times):
                totals = [None] * lines
                for who in range(2):
                    for lag in LAGS:
                        ref, pos = spans[who, time - lag]
                        value = ref[pos, band, :].astype(F32)
                        for line in range(lines):
                            row = (line * 2 + who) * len(LAGS) + lag - WIN
                            term = coef_ref[row : row + 1, :] * value
                            totals[line] = term if totals[line] is None else totals[line] + term
                for line in range(lines):
                    out = outs[number * lines + line]
                    out[index, band, :] = totals[line] if line == 0 else coded(totals[line])


def partials(coef, groups, lines, fields):
    trials, part = fields[0][2].shape[1:]
    outs = []
    for times in groups:
        shape = (len(times), trials, part)
        outs += [shaped(shape, F32)] + [shaped(shape, jnp.int16)] * (lines - 1)
    found = pl.pallas_call(
        functools.partial(partial_kernel, groups, lines, [field[:2] for field in fields]),
        out_shape=tuple(outs),
        in_specs=[VM] * (1 + len(fields)),
        out_specs=(VM,) * len(outs),
        compiler_params=params(),
        name="partials",
    )(coef, *[field[2] for field in fields])
    return [found[number * lines : (number + 1) * lines] for number in range(len(groups))]


def drive_kernel(own_ref, *refs):
    total = own_ref[...]
    for ref in refs[:-1]:
        total += decoded(ref[...])
    refs[-1][...] = total.astype(BF16).reshape(refs[-1].shape)


def drive_of(own, arrived):
    span, trials, part = own.shape
    return pl.pallas_call(
        drive_kernel,
        out_shape=shaped((span * trials, part), BF16),
        in_specs=[VM] * (1 + len(arrived)),
        out_specs=VM,
        compiler_params=params(),
        name="drive",
    )(own, *arrived)


def body(state_start, history, external, leak, w_rec, w_in, sources, delays, gains, proj_units):
    area = lax.axis_index("area").astype(jnp.int32).reshape(1)
    unit = lax.axis_index("unit").astype(jnp.int32).reshape(1)
    lines = lax.axis_size("area") // 2
    leak_row = leak.reshape(1, -1)

    facing = crossed(history, "area", 1)
    rates = jnp.tanh(state_start).astype(BF16)
    other = crossed(rates, "unit", 1)
    w_rec, w_in, history, external, leak_row, state, select, coef = stage(
        area, unit, (sources, delays, gains), proj_units, lines, (w_rec, w_in, history, external, leak_row, state_start)
    )
    known = [(0, -2 * WIN, history), (1, -2 * WIN, facing)]

    def send(groups):
        sent = []
        for sums in partials(coef, groups, lines, known):
            arrived = [crossed(sums[line], "area", 2 * line) for line in range(1, lines)]
            sent += [(sums[0], arrived)]
        return sent

    def drive_pair(group):
        own = drive_of(*group)
        return own, crossed(own, "unit", 1)

    groups = ((0,), tuple(range(1, WIN)))
    sent = send(groups)
    total, fresh = opening(unit, rates, other, w_rec, external, select)
    picks = [fresh]
    state, rates = first_step(unit, drive_pair(sent[0]), w_in, total, state, leak_row)

    drives = None
    for time in range(1, STEPS):
        other = crossed(rates, "unit", 1)
        early = time == WIN - 1
        if early:
            picks.append(pick(unit, rates, other, select))
            value = jnp.stack(picks)
            known += [(0, 0, value), (1, 0, crossed(value, "area", 1))]
        total, *half = own_part(unit, rates, w_rec, external, select, not early)
        if early:
            late = send(((WIN,), tuple(range(WIN + 1, STEPS))))
        half = None if early else half[0]
        if time == 1:
            drives, row = drive_pair(sent[1]), 0
        elif time < WIN:
            row = time - 1
        elif time == WIN:
            drives, row = drive_pair(late[0]), 0
        elif time == WIN + 1:
            drives, row = drive_pair(late[1]), 0
        else:
            row = time - WIN - 1
        common = (unit, other, w_rec, total, drives, row, w_in, state, leak_row, select, half)
        if time < STEPS - 1:
            state, rates, *fresh = step(*common)
            picks += fresh
    return last_step(*common, picks)


def wide_body(state_start, history, external, leak, w_rec, w_in, sources, delays, gains, proj_units):
    area_count = lax.axis_size("area")
    area_index = lax.axis_index("area")
    area_total = sources.shape[0]
    share = area_count // area_total
    own_area = area_index // share
    own_src = lax.dynamic_slice_in_dim(sources, own_area, 1, 0)[0]
    own_delay = lax.dynamic_slice_in_dim(delays, own_area, 1, 0)[0]
    own_gain = lax.dynamic_slice_in_dim(gains, own_area, 1, 0)[0]
    own_valid = own_src >= 0
    trial_count = state_start.shape[0]
    proj_part = proj_units.shape[0]
    unit_full = w_rec.shape[0]
    proj_full = w_in.shape[0]
    bit_count = share.bit_length() - 1
    select = (jnp.arange(unit_full, dtype=jnp.int32)[:, None] == proj_units[None, :]).astype(BF16)
    state_now = state_start
    received = []
    outgoing = history
    produced = []
    for window_idx in range(WINDOWS):
        move_span_len = outgoing.shape[0]
        flat = outgoing.reshape(1, -1)
        wanted = (own_src[:, None] * share + jnp.arange(share, dtype=jnp.int32)[None, :]).reshape(-1)
        piece = lax.all_gather(flat, "area", axis=0, tiled=True)
        count = piece.shape[0]
        match = wanted[:, None] == jnp.arange(count, dtype=jnp.int32)[None, :]
        total = jnp.dot(match.astype(BF16), piece, preferred_element_type=F32)
        received.append(
            total.astype(BF16).reshape(MAXSRC, share, move_span_len, trial_count, proj_part)
        )
        known = jnp.concatenate(received, axis=2)
        span_len = known.shape[2]
        times = window_idx * WIN + jnp.arange(WIN, dtype=jnp.int32)
        target_idx = times[:, None] - own_delay[None, :] + 2 * WIN
        columns = jnp.arange(span_len, dtype=jnp.int32)
        chosen_steps = (columns[None, None, :] == target_idx[:, :, None]) & own_valid[None, :, None]
        weight = jnp.where(chosen_steps, own_gain[None, :, None], jnp.float32(0.0))
        summed = jnp.einsum(
            "ikj,kqjbp->ibqp", weight, known.astype(F32), precision=lax.Precision.HIGHEST
        )
        drive_part = summed.astype(BF16)
        drive_full = lax.all_gather(drive_part[:, :, :, None, :], "unit", axis=3, tiled=True)
        current = jnp.dot(
            drive_full.reshape(WIN * trial_count, proj_full), w_in, preferred_element_type=F32
        )
        current = current.reshape(WIN, trial_count, -1)
        fresh = []
        for inner_step in range(WIN):
            rate_rows = jnp.tanh(state_now).astype(BF16)
            joined = lax.all_gather(rate_rows, "unit", axis=1, tiled=True)
            for bit in range(bit_count):
                other = swapped(joined, "area", bit)
                upper = area_index // (1 << bit) % 2 == 1
                joined = jnp.where(
                    upper,
                    jnp.concatenate([other, joined], axis=1),
                    jnp.concatenate([joined, other], axis=1),
                )
            recur = jnp.dot(joined, w_rec, preferred_element_type=F32)
            picked = jnp.dot(joined, select, preferred_element_type=F32)
            fresh.append(picked.astype(BF16))
            state_now = state_now + leak[None, :] * (
                -state_now + recur + current[inner_step] + external
            )
        outgoing = jnp.stack(fresh)
        produced.append(outgoing)
    return (state_now, jnp.concatenate(produced, axis=0))


def solution(mesh):
    split = P(None, ("groups", "area", "unit"))
    placed = (
        split,
        P(None, None, ("groups", "area", "unit")),
        split,
        P(("groups", "area", "unit")),
        split,
        split,
        P("groups", None),
        P("groups", None),
        P("groups", None),
        P(("groups", "area", "unit")),
    )

    def chosen(*args):
        areas = lax.axis_size("area")
        narrow = args[6].shape[0] == areas and lax.axis_size("unit") == 2 and areas & (areas - 1) == 0
        return (body if narrow else wide_body)(*args)

    return jax.shard_map(
        chosen,
        mesh=mesh,
        in_specs=placed,
        out_specs=(split, P(None, None, ("groups", "area", "unit"))),
        check_vma=False,
    )
```

```python
import functools

import jax
import jax.numpy as jnp
from jax import lax
from jax.experimental import pallas as pl
from jax.experimental.pallas import tpu as pltpu
from jax.sharding import PartitionSpec as P

MAXSRC = 6
WIN = 3
WINDOWS = 2
STEPS = WIN * WINDOWS
BF16 = jnp.bfloat16
F32 = jnp.float32
VM = pl.BlockSpec(memory_space=pltpu.VMEM)
SM = pl.BlockSpec(memory_space=pltpu.SMEM)
HB = pl.BlockSpec(memory_space=pltpu.MemorySpace.HBM)
LAGS = range(WIN, 2 * WIN + 1)
MIB = 1 << 20
CODE = 8192.0


def swapped(value, axis, stride):
    mask = 2**stride
    return crossed(value, axis, mask)


def crossed(value, axis, mask):
    pairs = [(source, source ^ mask) for source in range(lax.axis_size(axis))]
    return lax.ppermute(value, axis, pairs)


def shaped(shape, kind):
    return jax.ShapeDtypeStruct(shape, kind)


def params(limit=8):
    return pltpu.CompilerParams(vmem_limit_bytes=limit * MIB)


def columns_of(width):
    size = 256 if width % 256 == 0 else width
    return [slice(start, start + size) for start in range(0, width, size)]


def matmul(left, right):
    return jnp.dot(left, right, preferred_element_type=F32)


def far(array):
    return pltpu.with_memory_space_constraint(array, pltpu.MemorySpace.HBM)


def half_of(unit, count):
    return pl.ds(pl.multiple_of(unit * count, count), count)


def started(moves, sems):
    found = []
    for index, (source, target) in enumerate(moves):
        found.append(pltpu.make_async_copy(source, target, sems.at[index]))
        found[-1].start()
    return found


def stage_kernel(
    lines,
    area_ref,
    unit_ref,
    src_ref,
    delay_ref,
    gain_ref,
    units_ref,
    history_far,
    rec_far,
    in_far,
    history_ref,
    rec_ref,
    in_own_ref,
    in_other_ref,
    own_ref,
    other_ref,
    coef_ref,
    sems,
):
    area, unit = area_ref[0], unit_ref[0]
    count = rec_ref.shape[0]
    part = in_own_ref.shape[0]
    moves = started(
        [
            (history_far, history_ref),
            (rec_far.at[half_of(unit, count), :], rec_ref),
            (in_far.at[half_of(unit, part), :], in_own_ref),
            (in_far.at[half_of(1 - unit, part), :], in_other_ref),
        ],
        sems,
    )
    width = coef_ref.shape[1]
    row = 0
    for line in range(lines):
        target = area ^ (2 * line)
        for who in range(2):
            source = area ^ who
            delay, gain = jnp.int32(0), jnp.float32(0.0)
            for slot in range(MAXSRC):
                match = src_ref[target, slot] == source
                delay += jnp.where(match, delay_ref[target, slot], 0)
                gain += jnp.where(match, gain_ref[target, slot], 0.0)
            for lag in LAGS:
                value = jnp.where(delay == lag, gain, 0.0)
                coef_ref[row : row + 1, :] = jnp.full((1, width), value, F32)
                row += 1
    units = units_ref[...].reshape(1, width)
    for half, ref in ((unit, own_ref), (1 - unit, other_ref)):
        block = 256 if count % 256 == 0 else count
        for start in range(0, count, block):
            ids = lax.broadcasted_iota(jnp.int32, (block, width), 0) + (start + half * count)
            ref[start : start + block, :] = jnp.where(ids == units, 1.0, 0.0).astype(BF16)
    for move in moves:
        move.wait()


def stage(area, unit, tables, units, history, w_rec, w_in, lines):
    part = units.shape[0]
    count = w_rec.shape[0] // 2
    return pl.pallas_call(
        functools.partial(stage_kernel, lines),
        out_shape=(
            pltpu.VMEM(history.shape, BF16),
            pltpu.VMEM((count, w_rec.shape[1]), BF16),
            pltpu.VMEM((w_in.shape[0] // 2, w_in.shape[1]), BF16),
            pltpu.VMEM((w_in.shape[0] // 2, w_in.shape[1]), BF16),
            pltpu.VMEM((count, part), BF16),
            pltpu.VMEM((count, part), BF16),
            pltpu.VMEM((lines * 2 * len(LAGS), part), F32),
        ),
        in_specs=[SM] * 5 + [VM] + [HB] * 3,
        out_specs=(VM,) * 7,
        scratch_shapes=[pltpu.SemaphoreType.DMA((4,))],
        compiler_params=params(),
        name="stage",
    )(area, unit, *[far(table) for table in tables], far(units), far(history), far(w_rec), far(w_in))


def opening_kernel(
    unit_ref,
    rates_ref,
    facing_ref,
    own_ref,
    pick_own_ref,
    pick_other_ref,
    rec_far,
    extra_far,
    state_far,
    leak_far,
    other_ref,
    extra_ref,
    state_ref,
    leak_ref,
    out_ref,
    pick_ref,
    sems,
):
    unit = unit_ref[0]
    count = other_ref.shape[0]
    size = count // 2 if count % 512 == 0 else count
    spans = [slice(start, start + size) for start in range(0, count, size)]
    moves = [
        (rec_far.at[pl.ds(pl.multiple_of((1 - unit) * count + span.start, size), size), :], other_ref.at[span, :])
        for span in spans
    ]
    moves += [
        (extra_far, extra_ref),
        (state_far, state_ref),
        (leak_far, leak_ref),
    ]
    moves = started(moves, sems)
    for cols in columns_of(out_ref.shape[1]):
        out_ref[:, cols] = matmul(rates_ref[...], own_ref[:, cols])
    picked = matmul(rates_ref[...], pick_own_ref[...])
    picked += matmul(facing_ref[...], pick_other_ref[...])
    pick_ref[...] = picked.astype(BF16)
    for move, span in zip(moves, spans):
        move.wait()
        for cols in columns_of(out_ref.shape[1]):
            out_ref[:, cols] += matmul(facing_ref[:, span], other_ref[span, cols])
    for move in moves[len(spans) :]:
        move.wait()
    out_ref[...] += extra_ref[...]


def opening(unit, rates, facing, own, selects, w_rec, extra, state, leak):
    part = selects[0].shape[1]
    return pl.pallas_call(
        opening_kernel,
        out_shape=(
            pltpu.VMEM(own.shape, BF16),
            pltpu.VMEM(extra.shape, F32),
            pltpu.VMEM(state.shape, F32),
            pltpu.VMEM(leak.shape, F32),
            pltpu.VMEM(extra.shape, F32),
            pltpu.VMEM((rates.shape[0], part), BF16),
        ),
        in_specs=[SM] + [VM] * 5 + [HB] * 4,
        out_specs=(VM,) * 6,
        scratch_shapes=[pltpu.SemaphoreType.DMA((5,))],
        compiler_params=params(),
        name="opening",
    )(unit, rates, facing, own, *selects, *[far(array) for array in (w_rec, extra, state, leak)])


def pick_kernel(count, *refs):
    owns, others, (pick_own_ref, pick_other_ref, out_ref) = refs[:count], refs[count : 2 * count], refs[2 * count :]
    left = jnp.concatenate([ref[...] for ref in owns], axis=0)
    right = jnp.concatenate([ref[...] for ref in others], axis=0)
    picked = matmul(left, pick_own_ref[...]) + matmul(right, pick_other_ref[...])
    out_ref[...] = picked.astype(BF16).reshape(out_ref.shape)


def pick(pairs, selects):
    owns, others = zip(*pairs)
    return pl.pallas_call(
        functools.partial(pick_kernel, len(pairs)),
        out_shape=shaped((len(pairs), owns[0].shape[0], selects[0].shape[1]), BF16),
        in_specs=[VM] * (2 * len(pairs) + 2),
        out_specs=VM,
        compiler_params=params(),
        name="pick",
    )(*owns, *others, *selects)


def own_kernel(rates_ref, weight_ref, extra_ref, out_ref):
    for cols in columns_of(out_ref.shape[1]):
        out_ref[:, cols] = extra_ref[:, cols] + matmul(rates_ref[...], weight_ref[:, cols])


def own_part(rates, weight, extra):
    return pl.pallas_call(
        own_kernel,
        out_shape=shaped(extra.shape, F32),
        in_specs=[VM] * 3,
        out_specs=VM,
        compiler_params=params(),
        name="own_part",
    )(rates, weight, extra)


def renewed(cols, total, state_ref, leak_ref):
    state = state_ref[:, cols]
    return state + leak_ref[:, cols] * (total - state)


def step_kernel(flow, drives, last, sum_ref, state_ref, leak_ref, *refs):
    refs = list(refs)
    rates_ref, weight_ref = (refs.pop(0), refs.pop(0)) if flow else (None, None)
    if drives:
        d0_ref, d1_ref, i0_ref, i1_ref = (refs.pop(0) for _ in range(4))
    else:
        kept_ref = refs.pop(0)
    trials = state_ref.shape[0]
    moves = []

    def send(source, target):
        moves.append(pltpu.make_async_copy(source, target, sems.at[len(moves)]))
        moves[-1].start()

    if last:
        sems, state_buf, fresh, new_ref, all_ref = (refs.pop(index) for index in (-1, -1, -1, -2, -1))
        pick_own_ref, pick_other_ref, first_ref, second_ref = (refs.pop(0) for _ in range(4))
        count = len(refs) // 2
        old = 0
        for ref in (first_ref, second_ref):
            send(ref, all_ref.at[pl.ds(old, ref.shape[0])])
            old += ref.shape[0]
        left = jnp.concatenate([ref[...] for ref in refs[:count]], axis=0)
        right = jnp.concatenate([ref[...] for ref in refs[count:]], axis=0)
        picked = matmul(left, pick_own_ref[...]) + matmul(right, pick_other_ref[...])
        fresh[...] = picked.astype(BF16).reshape(fresh.shape)
        send(fresh, all_ref.at[pl.ds(old, fresh.shape[0])])
    else:
        state_buf, next_ref = refs[:2]
    for cols in columns_of(state_buf.shape[1]):
        total = sum_ref[:, cols]
        if flow:
            total += matmul(rates_ref[...], weight_ref[:, cols])
        if drives:
            current = matmul(d0_ref[...], i0_ref[:, cols]) + matmul(d1_ref[...], i1_ref[:, cols])
            refs[2][:, cols] = current[trials:, :]
            total += current[:trials, :]
        else:
            total += kept_ref[:, cols]
        state = renewed(cols, total, state_ref, leak_ref)
        state_buf[:, cols] = state
        if last:
            send(state_buf.at[:, cols], new_ref.at[:, cols])
        else:
            next_ref[:, cols] = jnp.tanh(state).astype(BF16)
    for move in moves:
        move.wait()


def step(total, state, leak, flow, drives, kept):
    outs = [shaped(state.shape, F32), shaped(state.shape, BF16)]
    given = list(flow or ())
    if drives:
        given += drives
        outs.append(shaped(state.shape, F32))
    else:
        given.append(kept)
    return pl.pallas_call(
        functools.partial(step_kernel, flow is not None, drives is not None, False),
        out_shape=tuple(outs),
        in_specs=[VM] * (3 + len(given)),
        out_specs=(VM,) * len(outs),
        compiler_params=params(),
        name="step",
    )(total, state, leak, *given)


def last_step(total, state, leak, flow, kept, selects, old, pairs):
    owns, others = zip(*pairs)
    trials, part = old[0].shape[1:]
    first = sum(value.shape[0] for value in old)
    given = [*flow, kept, *selects, *old, *owns, *others]
    return pl.pallas_call(
        functools.partial(step_kernel, True, False, True),
        out_shape=(shaped(state.shape, F32), shaped((first + len(pairs), trials, part), BF16)),
        in_specs=[VM] * (3 + len(given)),
        out_specs=(HB, HB),
        scratch_shapes=[
            pltpu.VMEM((len(pairs), trials, part), BF16),
            pltpu.VMEM(state.shape, F32),
            pltpu.SemaphoreType.DMA((len(old) + 1 + len(columns_of(state.shape[1])),)),
        ],
        compiler_params=params(),
        name="last_step",
    )(total, state, leak, *given)


def coded(value):
    return jnp.round(value * CODE).astype(jnp.int32).astype(jnp.int16)


def decoded(value):
    return value.astype(jnp.int32).astype(F32) * (1.0 / CODE)


def partial_kernel(times, lines, slots, coef_ref, *refs):
    fields, outs = refs[: len(slots)], refs[len(slots) :]
    trials = fields[0].shape[-2]
    size = 16 if trials % 16 == 0 else trials
    spans = {}
    for ref, (who, first) in zip(fields, slots):
        for pos in range(ref.shape[0]):
            spans[who, first + pos] = (ref, pos)
    for start in range(0, trials, size):
        band = slice(start, start + size)
        for index, time in enumerate(times):
            totals = [None] * lines
            for who in range(2):
                for lag in LAGS:
                    ref, pos = spans[who, time - lag]
                    value = ref[pos, band, :].astype(F32)
                    for line in range(lines):
                        row = (line * 2 + who) * len(LAGS) + lag - WIN
                        term = coef_ref[row : row + 1, :] * value
                        totals[line] = term if totals[line] is None else totals[line] + term
            for line in range(lines):
                outs[line][index, band, :] = totals[line] if line == 0 else coded(totals[line])


def partials(coef, times, lines, fields):
    shape = (len(times),) + fields[0][2].shape[1:]
    outs = [shaped(shape, F32)] + [shaped(shape, jnp.int16)] * (lines - 1)
    return pl.pallas_call(
        functools.partial(partial_kernel, times, lines, [field[:2] for field in fields]),
        out_shape=tuple(outs),
        in_specs=[VM] * (1 + len(fields)),
        out_specs=(VM,) * len(outs),
        compiler_params=params(),
        name="partials",
    )(coef, *[field[2] for field in fields])


def drive_kernel(own_ref, *refs):
    total = own_ref[...]
    for ref in refs[:-1]:
        total += decoded(ref[...])
    refs[-1][...] = total.astype(BF16).reshape(refs[-1].shape)


def drive_of(own, arrived):
    span, trials, part = own.shape
    return pl.pallas_call(
        drive_kernel,
        out_shape=shaped((span * trials, part), BF16),
        in_specs=[VM] * (1 + len(arrived)),
        out_specs=VM,
        compiler_params=params(),
        name="drive",
    )(own, *arrived)


def body(*args):
    return narrow_body(*args)


def narrow_body(state_start, history, external, leak, w_rec, w_in, sources, delays, gains, proj_units):
    area = lax.axis_index("area").astype(jnp.int32).reshape(1)
    unit = lax.axis_index("unit").astype(jnp.int32).reshape(1)
    lines = lax.axis_size("area") // 2
    leak_row = leak.reshape(1, -1)

    facing = crossed(history, "area", 1)
    rates = jnp.tanh(state_start).astype(BF16)
    other = crossed(rates, "unit", 1)
    history, rec_own, in_own, in_other, select_own, select_other, coef = stage(
        area, unit, (sources, delays, gains), proj_units, history, w_rec, w_in, lines
    )
    selects = (select_own, select_other)
    known = [(0, -2 * WIN, history), (1, -2 * WIN, facing)]

    def send(times):
        sums = partials(coef, times, lines, known)
        arrived = []
        for line in range(1, lines):
            arrived.append(crossed(sums[line], "area", 2 * line))
        return sums[0], arrived

    def drive_pair(group):
        own = drive_of(*group)
        return [own, crossed(own, "unit", 1), in_own, in_other]

    def share(value, first):
        return [(0, first, value), (1, first, crossed(value, "area", 1))]

    sent = send((0, 1))
    rec_other, external, state, leak_row, total, fresh = opening(
        unit, rates, other, rec_own, selects, w_rec, external, state_start, leak_row
    )
    known += share(fresh[None], 0)
    old, pairs, flow, kept = [fresh[None]], [], None, None
    for time in range(STEPS):
        if time > 0:
            other = crossed(rates, "unit", 1)
            pairs.append((rates, other))
            flow = (other, rec_other)
            if time == 2:
                fresh = pick(pairs, selects)
                old.append(fresh)
                pairs = []
                known += share(fresh, 1)
            total = own_part(rates, rec_own, external)
        if time == STEPS - 1:
            return last_step(total, state, leak_row, flow, kept, selects, old, pairs)
        drives = drive_pair(sent) if time % 2 == 0 else None
        if time in (0, 2):
            sent = send((time + 2, time + 3))
        state, rates, *more = step(total, state, leak_row, flow, drives, kept)
        kept = more[0] if more else None


def wide_body(state_start, history, external, leak, w_rec, w_in, sources, delays, gains, proj_units):
    area_count = lax.axis_size("area")
    area_index = lax.axis_index("area")
    area_total = sources.shape[0]
    share = area_count // area_total
    own_area = area_index // share
    own_src = lax.dynamic_slice_in_dim(sources, own_area, 1, 0)[0]
    own_delay = lax.dynamic_slice_in_dim(delays, own_area, 1, 0)[0]
    own_gain = lax.dynamic_slice_in_dim(gains, own_area, 1, 0)[0]
    own_valid = own_src >= 0
    trial_count = state_start.shape[0]
    proj_part = proj_units.shape[0]
    unit_full = w_rec.shape[0]
    proj_full = w_in.shape[0]
    bit_count = share.bit_length() - 1
    select = (jnp.arange(unit_full, dtype=jnp.int32)[:, None] == proj_units[None, :]).astype(BF16)
    state_now = state_start
    received = []
    outgoing = history
    produced = []
    for window_idx in range(WINDOWS):
        move_span_len = outgoing.shape[0]
        flat = outgoing.reshape(1, -1)
        wanted = (own_src[:, None] * share + jnp.arange(share, dtype=jnp.int32)[None, :]).reshape(-1)
        piece = lax.all_gather(flat, "area", axis=0, tiled=True)
        count = piece.shape[0]
        match = wanted[:, None] == jnp.arange(count, dtype=jnp.int32)[None, :]
        total = jnp.dot(match.astype(BF16), piece, preferred_element_type=F32)
        received.append(
            total.astype(BF16).reshape(MAXSRC, share, move_span_len, trial_count, proj_part)
        )
        known = jnp.concatenate(received, axis=2)
        span_len = known.shape[2]
        times = window_idx * WIN + jnp.arange(WIN, dtype=jnp.int32)
        target_idx = times[:, None] - own_delay[None, :] + 2 * WIN
        columns = jnp.arange(span_len, dtype=jnp.int32)
        chosen_steps = (columns[None, None, :] == target_idx[:, :, None]) & own_valid[None, :, None]
        weight = jnp.where(chosen_steps, own_gain[None, :, None], jnp.float32(0.0))
        summed = jnp.einsum(
            "ikj,kqjbp->ibqp", weight, known.astype(F32), precision=lax.Precision.HIGHEST
        )
        drive_part = summed.astype(BF16)
        drive_full = lax.all_gather(drive_part[:, :, :, None, :], "unit", axis=3, tiled=True)
        current = jnp.dot(
            drive_full.reshape(WIN * trial_count, proj_full), w_in, preferred_element_type=F32
        )
        current = current.reshape(WIN, trial_count, -1)
        fresh = []
        for inner_step in range(WIN):
            rate_rows = jnp.tanh(state_now).astype(BF16)
            joined = lax.all_gather(rate_rows, "unit", axis=1, tiled=True)
            for bit in range(bit_count):
                other = swapped(joined, "area", bit)
                upper = area_index // (1 << bit) % 2 == 1
                joined = jnp.where(
                    upper,
                    jnp.concatenate([other, joined], axis=1),
                    jnp.concatenate([joined, other], axis=1),
                )
            recur = jnp.dot(joined, w_rec, preferred_element_type=F32)
            picked = jnp.dot(joined, select, preferred_element_type=F32)
            fresh.append(picked.astype(BF16))
            state_now = state_now + leak[None, :] * (
                -state_now + recur + current[inner_step] + external
            )
        outgoing = jnp.stack(fresh)
        produced.append(outgoing)
    return (state_now, jnp.concatenate(produced, axis=0))


def solution(mesh):
    split = P(None, ("groups", "area", "unit"))
    placed = (
        split,
        P(None, None, ("groups", "area", "unit")),
        split,
        P(("groups", "area", "unit")),
        split,
        split,
        P("groups", None),
        P("groups", None),
        P("groups", None),
        P(("groups", "area", "unit")),
    )

    def chosen(*args):
        areas = lax.axis_size("area")
        narrow = args[6].shape[0] == areas and lax.axis_size("unit") == 2 and areas & (areas - 1) == 0
        return (body if narrow else wide_body)(*args)

    return jax.shard_map(
        chosen,
        mesh=mesh,
        in_specs=placed,
        out_specs=(split, P(None, None, ("groups", "area", "unit"))),
        check_vma=False,
    )
```

```python
import functools

import jax
import jax.numpy as jnp
from jax import lax
from jax.experimental import pallas as pl
from jax.experimental.pallas import tpu as pltpu
from jax.sharding import PartitionSpec as P

MAXSRC = 6
WIN = 3
WINDOWS = 2
STEPS = WIN * WINDOWS
BF16 = jnp.bfloat16
F32 = jnp.float32
VM = pl.BlockSpec(memory_space=pltpu.VMEM)
SM = pl.BlockSpec(memory_space=pltpu.SMEM)
HB = pl.BlockSpec(memory_space=pltpu.MemorySpace.HBM)
LAGS = range(WIN, 2 * WIN + 1)
MIB = 1 << 20
CODE = 8192.0


def swapped(value, axis, stride):
    mask = 2**stride
    return crossed(value, axis, mask)


def crossed(value, axis, mask):
    pairs = [(source, source ^ mask) for source in range(lax.axis_size(axis))]
    return lax.ppermute(value, axis, pairs)


def shaped(shape, kind):
    return jax.ShapeDtypeStruct(shape, kind)


def params(limit=8):
    return pltpu.CompilerParams(vmem_limit_bytes=limit * MIB)


def columns_of(width):
    size = 256 if width % 256 == 0 else width
    return [slice(start, start + size) for start in range(0, width, size)]


def matmul(left, right):
    return jnp.dot(left, right, preferred_element_type=F32)


def far(array):
    return pltpu.with_memory_space_constraint(array, pltpu.MemorySpace.HBM)


def half_of(unit, count):
    return pl.ds(pl.multiple_of(unit * count, count), count)


def started(moves, sems):
    found = []
    for index, (source, target) in enumerate(moves):
        found.append(pltpu.make_async_copy(source, target, sems.at[index]))
        found[-1].start()
    return found


def stage_kernel(
    lines,
    area_ref,
    unit_ref,
    src_ref,
    delay_ref,
    gain_ref,
    units_ref,
    history_far,
    rec_far,
    in_far,
    history_ref,
    rec_ref,
    in_own_ref,
    in_other_ref,
    own_ref,
    other_ref,
    coef_ref,
    sems,
):
    area, unit = area_ref[0], unit_ref[0]
    count = rec_ref.shape[0]
    part = in_own_ref.shape[0]
    moves = started(
        [
            (history_far, history_ref),
            (rec_far.at[half_of(unit, count), :], rec_ref),
            (in_far.at[half_of(unit, part), :], in_own_ref),
            (in_far.at[half_of(1 - unit, part), :], in_other_ref),
        ],
        sems,
    )
    width = coef_ref.shape[1]
    row = 0
    for line in range(lines):
        target = area ^ (2 * line)
        for who in range(2):
            source = area ^ who
            delay, gain = jnp.int32(0), jnp.float32(0.0)
            for slot in range(MAXSRC):
                match = src_ref[target, slot] == source
                delay += jnp.where(match, delay_ref[target, slot], 0)
                gain += jnp.where(match, gain_ref[target, slot], 0.0)
            for lag in LAGS:
                value = jnp.where(delay == lag, gain, 0.0)
                coef_ref[row : row + 1, :] = jnp.full((1, width), value, F32)
                row += 1
    units = units_ref[...].reshape(1, width)
    for half, ref in ((unit, own_ref), (1 - unit, other_ref)):
        block = 256 if count % 256 == 0 else count
        for start in range(0, count, block):
            ids = lax.broadcasted_iota(jnp.int32, (block, width), 0) + (start + half * count)
            ref[start : start + block, :] = jnp.where(ids == units, 1.0, 0.0).astype(BF16)
    for move in moves:
        move.wait()


def stage(area, unit, tables, units, history, w_rec, w_in, lines):
    part = units.shape[0]
    count = w_rec.shape[0] // 2
    return pl.pallas_call(
        functools.partial(stage_kernel, lines),
        out_shape=(
            pltpu.VMEM(history.shape, BF16),
            pltpu.VMEM((count, w_rec.shape[1]), BF16),
            pltpu.VMEM((w_in.shape[0] // 2, w_in.shape[1]), BF16),
            pltpu.VMEM((w_in.shape[0] // 2, w_in.shape[1]), BF16),
            pltpu.VMEM((count, part), BF16),
            pltpu.VMEM((count, part), BF16),
            pltpu.VMEM((lines * 2 * len(LAGS), part), F32),
        ),
        in_specs=[SM] * 5 + [VM] + [HB] * 3,
        out_specs=(VM,) * 7,
        scratch_shapes=[pltpu.SemaphoreType.DMA((4,))],
        compiler_params=params(),
        name="stage",
    )(area, unit, *[far(table) for table in tables], far(units), far(history), far(w_rec), far(w_in))


def opening_kernel(
    unit_ref,
    rates_ref,
    facing_ref,
    own_ref,
    rec_far,
    extra_far,
    state_far,
    leak_far,
    other_ref,
    extra_ref,
    state_ref,
    leak_ref,
    out_ref,
    sems,
):
    unit = unit_ref[0]
    count = other_ref.shape[0]
    size = count // 2 if count % 512 == 0 else count
    spans = [slice(start, start + size) for start in range(0, count, size)]
    moves = [
        (rec_far.at[pl.ds(pl.multiple_of((1 - unit) * count + span.start, size), size), :], other_ref.at[span, :])
        for span in spans
    ]
    moves += [
        (extra_far, extra_ref),
        (state_far, state_ref),
        (leak_far, leak_ref),
    ]
    moves = started(moves, sems)
    for cols in columns_of(out_ref.shape[1]):
        out_ref[:, cols] = matmul(rates_ref[...], own_ref[:, cols])
    for move, span in zip(moves, spans):
        move.wait()
        for cols in columns_of(out_ref.shape[1]):
            out_ref[:, cols] += matmul(facing_ref[:, span], other_ref[span, cols])
    for move in moves[len(spans) :]:
        move.wait()
    out_ref[...] += extra_ref[...]


def opening(unit, rates, facing, own, w_rec, extra, state, leak):
    return pl.pallas_call(
        opening_kernel,
        out_shape=(
            pltpu.VMEM(own.shape, BF16),
            pltpu.VMEM(extra.shape, F32),
            pltpu.VMEM(state.shape, F32),
            pltpu.VMEM(leak.shape, F32),
            pltpu.VMEM(extra.shape, F32),
        ),
        in_specs=[SM] + [VM] * 3 + [HB] * 4,
        out_specs=(VM,) * 5,
        scratch_shapes=[pltpu.SemaphoreType.DMA((5,))],
        compiler_params=params(),
        name="opening",
    )(unit, rates, facing, own, *[far(array) for array in (w_rec, extra, state, leak)])


def pick_kernel(count, *refs):
    owns, others, (pick_own_ref, pick_other_ref, out_ref) = refs[:count], refs[count : 2 * count], refs[2 * count :]
    left = jnp.concatenate([ref[...] for ref in owns], axis=0)
    right = jnp.concatenate([ref[...] for ref in others], axis=0)
    picked = matmul(left, pick_own_ref[...]) + matmul(right, pick_other_ref[...])
    out_ref[...] = picked.astype(BF16).reshape(out_ref.shape)


def pick(pairs, selects):
    owns, others = zip(*pairs)
    return pl.pallas_call(
        functools.partial(pick_kernel, len(pairs)),
        out_shape=shaped((len(pairs), owns[0].shape[0], selects[0].shape[1]), BF16),
        in_specs=[VM] * (2 * len(pairs) + 2),
        out_specs=VM,
        compiler_params=params(),
        name="pick",
    )(*owns, *others, *selects)


def own_kernel(rates_ref, weight_ref, extra_ref, out_ref):
    for cols in columns_of(out_ref.shape[1]):
        out_ref[:, cols] = extra_ref[:, cols] + matmul(rates_ref[...], weight_ref[:, cols])


def own_part(rates, weight, extra):
    return pl.pallas_call(
        own_kernel,
        out_shape=shaped(extra.shape, F32),
        in_specs=[VM] * 3,
        out_specs=VM,
        compiler_params=params(),
        name="own_part",
    )(rates, weight, extra)


def renewed(cols, total, state_ref, leak_ref):
    state = state_ref[:, cols]
    return state + leak_ref[:, cols] * (total - state)


def step_kernel(flow, drives, last, sum_ref, state_ref, leak_ref, *refs):
    refs = list(refs)
    rates_ref, weight_ref = (refs.pop(0), refs.pop(0)) if flow else (None, None)
    if drives:
        d0_ref, d1_ref, i0_ref, i1_ref = (refs.pop(0) for _ in range(4))
    else:
        kept_ref = refs.pop(0)
    trials = state_ref.shape[0]
    moves = []

    def send(source, target):
        moves.append(pltpu.make_async_copy(source, target, sems.at[len(moves)]))
        moves[-1].start()

    if last:
        sems, state_buf, fresh, new_ref, all_ref = (refs.pop(index) for index in (-1, -1, -1, -2, -1))
        pick_own_ref, pick_other_ref, first_ref, second_ref = (refs.pop(0) for _ in range(4))
        count = len(refs) // 2
        old = 0
        for ref in (first_ref, second_ref):
            send(ref, all_ref.at[pl.ds(old, ref.shape[0])])
            old += ref.shape[0]
        left = jnp.concatenate([ref[...] for ref in refs[:count]], axis=0)
        right = jnp.concatenate([ref[...] for ref in refs[count:]], axis=0)
        picked = matmul(left, pick_own_ref[...]) + matmul(right, pick_other_ref[...])
        fresh[...] = picked.astype(BF16).reshape(fresh.shape)
        send(fresh, all_ref.at[pl.ds(old, fresh.shape[0])])
    else:
        state_buf, next_ref = refs[:2]
    for cols in columns_of(state_buf.shape[1]):
        total = sum_ref[:, cols]
        if flow:
            total += matmul(rates_ref[...], weight_ref[:, cols])
        if drives:
            current = matmul(d0_ref[...], i0_ref[:, cols]) + matmul(d1_ref[...], i1_ref[:, cols])
            refs[2][:, cols] = current[trials:, :]
            total += current[:trials, :]
        else:
            total += kept_ref[:, cols]
        state = renewed(cols, total, state_ref, leak_ref)
        state_buf[:, cols] = state
        if last:
            send(state_buf.at[:, cols], new_ref.at[:, cols])
        else:
            next_ref[:, cols] = jnp.tanh(state).astype(BF16)
    for move in moves:
        move.wait()


def step(total, state, leak, flow, drives, kept):
    outs = [shaped(state.shape, F32), shaped(state.shape, BF16)]
    given = list(flow or ())
    if drives:
        given += drives
        outs.append(shaped(state.shape, F32))
    else:
        given.append(kept)
    return pl.pallas_call(
        functools.partial(step_kernel, flow is not None, drives is not None, False),
        out_shape=tuple(outs),
        in_specs=[VM] * (3 + len(given)),
        out_specs=(VM,) * len(outs),
        compiler_params=params(),
        name="step",
    )(total, state, leak, *given)


def last_step(total, state, leak, flow, kept, selects, old, pairs):
    owns, others = zip(*pairs)
    trials, part = old[0].shape[1:]
    first = sum(value.shape[0] for value in old)
    given = [*flow, kept, *selects, *old, *owns, *others]
    return pl.pallas_call(
        functools.partial(step_kernel, True, False, True),
        out_shape=(shaped(state.shape, F32), shaped((first + len(pairs), trials, part), BF16)),
        in_specs=[VM] * (3 + len(given)),
        out_specs=(HB, HB),
        scratch_shapes=[
            pltpu.VMEM((len(pairs), trials, part), BF16),
            pltpu.VMEM(state.shape, F32),
            pltpu.SemaphoreType.DMA((len(old) + 1 + len(columns_of(state.shape[1])),)),
        ],
        compiler_params=params(),
        name="last_step",
    )(total, state, leak, *given)


def coded(value):
    return jnp.round(value * CODE).astype(jnp.int32).astype(jnp.int16)


def decoded(value):
    return value.astype(jnp.int32).astype(F32) * (1.0 / CODE)


def partial_kernel(times, lines, slots, coef_ref, *refs):
    fields, outs = refs[: len(slots)], refs[len(slots) :]
    trials = fields[0].shape[-2]
    size = 16 if trials % 16 == 0 else trials
    spans = {}
    for ref, (who, first) in zip(fields, slots):
        for pos in range(ref.shape[0]):
            spans[who, first + pos] = (ref, pos)
    for start in range(0, trials, size):
        band = slice(start, start + size)
        for index, time in enumerate(times):
            totals = [None] * lines
            for who in range(2):
                for lag in LAGS:
                    ref, pos = spans[who, time - lag]
                    value = ref[pos, band, :].astype(F32)
                    for line in range(lines):
                        row = (line * 2 + who) * len(LAGS) + lag - WIN
                        term = coef_ref[row : row + 1, :] * value
                        totals[line] = term if totals[line] is None else totals[line] + term
            for line in range(lines):
                outs[line][index, band, :] = totals[line] if line == 0 else coded(totals[line])


def partials(coef, times, lines, fields):
    shape = (len(times),) + fields[0][2].shape[1:]
    outs = [shaped(shape, F32)] + [shaped(shape, jnp.int16)] * (lines - 1)
    return pl.pallas_call(
        functools.partial(partial_kernel, times, lines, [field[:2] for field in fields]),
        out_shape=tuple(outs),
        in_specs=[VM] * (1 + len(fields)),
        out_specs=(VM,) * len(outs),
        compiler_params=params(),
        name="partials",
    )(coef, *[field[2] for field in fields])


def drive_kernel(own_ref, *refs):
    total = own_ref[...]
    for ref in refs[:-1]:
        total += decoded(ref[...])
    refs[-1][...] = total.astype(BF16).reshape(refs[-1].shape)


def drive_of(own, arrived):
    span, trials, part = own.shape
    return pl.pallas_call(
        drive_kernel,
        out_shape=shaped((span * trials, part), BF16),
        in_specs=[VM] * (1 + len(arrived)),
        out_specs=VM,
        compiler_params=params(),
        name="drive",
    )(own, *arrived)


def body(*args):
    return narrow_body(*args)


def narrow_body(state_start, history, external, leak, w_rec, w_in, sources, delays, gains, proj_units):
    area = lax.axis_index("area").astype(jnp.int32).reshape(1)
    unit = lax.axis_index("unit").astype(jnp.int32).reshape(1)
    lines = lax.axis_size("area") // 2
    leak_row = leak.reshape(1, -1)

    facing = crossed(history, "area", 1)
    rates = jnp.tanh(state_start).astype(BF16)
    other = crossed(rates, "unit", 1)
    history, rec_own, in_own, in_other, select_own, select_other, coef = stage(
        area, unit, (sources, delays, gains), proj_units, history, w_rec, w_in, lines
    )
    selects = (select_own, select_other)
    known = [(0, -2 * WIN, history), (1, -2 * WIN, facing)]

    def send(times):
        sums = partials(coef, times, lines, known)
        arrived = []
        for line in range(1, lines):
            arrived.append(crossed(sums[line], "area", 2 * line))
        return sums[0], arrived

    def drive_pair(group):
        own = drive_of(*group)
        return [own, crossed(own, "unit", 1), in_own, in_other]

    def share(value, first):
        return [(0, first, value), (1, first, crossed(value, "area", 1))]

    fresh = pick([(rates, other)], selects)
    sent = send((0, 1))
    known += share(fresh, 0)
    rec_other, external, state, leak_row, total = opening(
        unit, rates, other, rec_own, w_rec, external, state_start, leak_row
    )
    old, pairs, flow, kept = [fresh], [], None, None
    for time in range(STEPS):
        if time > 0:
            other = crossed(rates, "unit", 1)
            pairs.append((rates, other))
            flow = (other, rec_other)
            if time == 2:
                fresh = pick(pairs, selects)
                old.append(fresh)
                pairs = []
                known += share(fresh, 1)
            total = own_part(rates, rec_own, external)
        if time == STEPS - 1:
            return last_step(total, state, leak_row, flow, kept, selects, old, pairs)
        drives = drive_pair(sent) if time % 2 == 0 else None
        if time in (0, 2):
            sent = send((time + 2, time + 3))
        state, rates, *more = step(total, state, leak_row, flow, drives, kept)
        kept = more[0] if more else None


def wide_body(state_start, history, external, leak, w_rec, w_in, sources, delays, gains, proj_units):
    area_count = lax.axis_size("area")
    area_index = lax.axis_index("area")
    area_total = sources.shape[0]
    share = area_count // area_total
    own_area = area_index // share
    own_src = lax.dynamic_slice_in_dim(sources, own_area, 1, 0)[0]
    own_delay = lax.dynamic_slice_in_dim(delays, own_area, 1, 0)[0]
    own_gain = lax.dynamic_slice_in_dim(gains, own_area, 1, 0)[0]
    own_valid = own_src >= 0
    trial_count = state_start.shape[0]
    proj_part = proj_units.shape[0]
    unit_full = w_rec.shape[0]
    proj_full = w_in.shape[0]
    bit_count = share.bit_length() - 1
    select = (jnp.arange(unit_full, dtype=jnp.int32)[:, None] == proj_units[None, :]).astype(BF16)
    state_now = state_start
    received = []
    outgoing = history
    produced = []
    for window_idx in range(WINDOWS):
        move_span_len = outgoing.shape[0]
        flat = outgoing.reshape(1, -1)
        wanted = (own_src[:, None] * share + jnp.arange(share, dtype=jnp.int32)[None, :]).reshape(-1)
        piece = lax.all_gather(flat, "area", axis=0, tiled=True)
        count = piece.shape[0]
        match = wanted[:, None] == jnp.arange(count, dtype=jnp.int32)[None, :]
        total = jnp.dot(match.astype(BF16), piece, preferred_element_type=F32)
        received.append(
            total.astype(BF16).reshape(MAXSRC, share, move_span_len, trial_count, proj_part)
        )
        known = jnp.concatenate(received, axis=2)
        span_len = known.shape[2]
        times = window_idx * WIN + jnp.arange(WIN, dtype=jnp.int32)
        target_idx = times[:, None] - own_delay[None, :] + 2 * WIN
        columns = jnp.arange(span_len, dtype=jnp.int32)
        chosen_steps = (columns[None, None, :] == target_idx[:, :, None]) & own_valid[None, :, None]
        weight = jnp.where(chosen_steps, own_gain[None, :, None], jnp.float32(0.0))
        summed = jnp.einsum(
            "ikj,kqjbp->ibqp", weight, known.astype(F32), precision=lax.Precision.HIGHEST
        )
        drive_part = summed.astype(BF16)
        drive_full = lax.all_gather(drive_part[:, :, :, None, :], "unit", axis=3, tiled=True)
        current = jnp.dot(
            drive_full.reshape(WIN * trial_count, proj_full), w_in, preferred_element_type=F32
        )
        current = current.reshape(WIN, trial_count, -1)
        fresh = []
        for inner_step in range(WIN):
            rate_rows = jnp.tanh(state_now).astype(BF16)
            joined = lax.all_gather(rate_rows, "unit", axis=1, tiled=True)
            for bit in range(bit_count):
                other = swapped(joined, "area", bit)
                upper = area_index // (1 << bit) % 2 == 1
                joined = jnp.where(
                    upper,
                    jnp.concatenate([other, joined], axis=1),
                    jnp.concatenate([joined, other], axis=1),
                )
            recur = jnp.dot(joined, w_rec, preferred_element_type=F32)
            picked = jnp.dot(joined, select, preferred_element_type=F32)
            fresh.append(picked.astype(BF16))
            state_now = state_now + leak[None, :] * (
                -state_now + recur + current[inner_step] + external
            )
        outgoing = jnp.stack(fresh)
        produced.append(outgoing)
    return (state_now, jnp.concatenate(produced, axis=0))


def solution(mesh):
    split = P(None, ("groups", "area", "unit"))
    placed = (
        split,
        P(None, None, ("groups", "area", "unit")),
        split,
        P(("groups", "area", "unit")),
        split,
        split,
        P("groups", None),
        P("groups", None),
        P("groups", None),
        P(("groups", "area", "unit")),
    )

    def chosen(*args):
        areas = lax.axis_size("area")
        narrow = args[6].shape[0] == areas and lax.axis_size("unit") == 2 and areas & (areas - 1) == 0
        return (body if narrow else wide_body)(*args)

    return jax.shard_map(
        chosen,
        mesh=mesh,
        in_specs=placed,
        out_specs=(split, P(None, None, ("groups", "area", "unit"))),
        check_vma=False,
    )
```

```python
import functools

import jax
import jax.numpy as jnp
from jax import lax
from jax.experimental import pallas as pl
from jax.experimental.pallas import tpu as pltpu
from jax.sharding import PartitionSpec as P

MAXSRC = 6
WIN = 3
WINDOWS = 2
STEPS = WIN * WINDOWS
BF16 = jnp.bfloat16
F32 = jnp.float32
VM = pl.BlockSpec(memory_space=pltpu.VMEM)
SM = pl.BlockSpec(memory_space=pltpu.SMEM)
HB = pl.BlockSpec(memory_space=pltpu.MemorySpace.HBM)
LAGS = range(WIN, 2 * WIN + 1)
MIB = 1 << 20
CODE = 8192.0


def swapped(value, axis, stride):
    mask = 2**stride
    return crossed(value, axis, mask)


def crossed(value, axis, mask):
    pairs = [(source, source ^ mask) for source in range(lax.axis_size(axis))]
    return lax.ppermute(value, axis, pairs)


def shaped(shape, kind):
    return jax.ShapeDtypeStruct(shape, kind)


def params(limit=8):
    return pltpu.CompilerParams(vmem_limit_bytes=limit * MIB)


def columns_of(width):
    size = 256 if width % 256 == 0 else width
    return [slice(start, start + size) for start in range(0, width, size)]


def matmul(left, right):
    return jnp.dot(left, right, preferred_element_type=F32)


def far(array):
    return pltpu.with_memory_space_constraint(array, pltpu.MemorySpace.HBM)


def half_of(unit, count):
    return pl.ds(pl.multiple_of(unit * count, count), count)


def started(moves, sems):
    found = []
    for index, (source, target) in enumerate(moves):
        found.append(pltpu.make_async_copy(source, target, sems.at[index]))
        found[-1].start()
    return found


def stage_kernel(
    lines,
    area_ref,
    unit_ref,
    src_ref,
    delay_ref,
    gain_ref,
    units_ref,
    history_far,
    rec_far,
    in_far,
    history_ref,
    rec_ref,
    in_own_ref,
    in_other_ref,
    own_ref,
    other_ref,
    coef_ref,
    sems,
):
    area, unit = area_ref[0], unit_ref[0]
    count = rec_ref.shape[0]
    part = in_own_ref.shape[0]
    moves = started(
        [
            (history_far, history_ref),
            (rec_far.at[half_of(unit, count), :], rec_ref),
            (in_far.at[half_of(unit, part), :], in_own_ref),
            (in_far.at[half_of(1 - unit, part), :], in_other_ref),
        ],
        sems,
    )
    width = coef_ref.shape[1]
    row = 0
    for line in range(lines):
        target = area ^ (2 * line)
        for who in range(2):
            source = area ^ who
            delay, gain = jnp.int32(0), jnp.float32(0.0)
            for slot in range(MAXSRC):
                match = src_ref[target, slot] == source
                delay += jnp.where(match, delay_ref[target, slot], 0)
                gain += jnp.where(match, gain_ref[target, slot], 0.0)
            for lag in LAGS:
                value = jnp.where(delay == lag, gain, 0.0)
                coef_ref[row : row + 1, :] = jnp.full((1, width), value, F32)
                row += 1
    units = units_ref[...].reshape(1, width)
    for half, ref in ((unit, own_ref), (1 - unit, other_ref)):
        block = 256 if count % 256 == 0 else count
        for start in range(0, count, block):
            ids = lax.broadcasted_iota(jnp.int32, (block, width), 0) + (start + half * count)
            ref[start : start + block, :] = jnp.where(ids == units, 1.0, 0.0).astype(BF16)
    for move in moves:
        move.wait()


def stage(area, unit, tables, units, history, w_rec, w_in, lines):
    part = units.shape[0]
    count = w_rec.shape[0] // 2
    return pl.pallas_call(
        functools.partial(stage_kernel, lines),
        out_shape=(
            pltpu.VMEM(history.shape, BF16),
            pltpu.VMEM((count, w_rec.shape[1]), BF16),
            pltpu.VMEM((w_in.shape[0] // 2, w_in.shape[1]), BF16),
            pltpu.VMEM((w_in.shape[0] // 2, w_in.shape[1]), BF16),
            pltpu.VMEM((count, part), BF16),
            pltpu.VMEM((count, part), BF16),
            pltpu.VMEM((lines * 2 * len(LAGS), part), F32),
        ),
        in_specs=[SM] * 5 + [VM] + [HB] * 3,
        out_specs=(VM,) * 7,
        scratch_shapes=[pltpu.SemaphoreType.DMA((4,))],
        compiler_params=params(),
        name="stage",
    )(area, unit, *[far(table) for table in tables], far(units), far(history), far(w_rec), far(w_in))


def opening_kernel(
    unit_ref,
    rates_ref,
    facing_ref,
    own_ref,
    rec_far,
    extra_far,
    state_far,
    leak_far,
    other_ref,
    extra_ref,
    state_ref,
    leak_ref,
    out_ref,
    sems,
):
    unit = unit_ref[0]
    count = other_ref.shape[0]
    size = count // 2 if count % 512 == 0 else count
    spans = [slice(start, start + size) for start in range(0, count, size)]
    moves = [
        (rec_far.at[pl.ds(pl.multiple_of((1 - unit) * count + span.start, size), size), :], other_ref.at[span, :])
        for span in spans
    ]
    moves += [
        (extra_far, extra_ref),
        (state_far, state_ref),
        (leak_far, leak_ref),
    ]
    moves = started(moves, sems)
    for cols in columns_of(out_ref.shape[1]):
        out_ref[:, cols] = matmul(rates_ref[...], own_ref[:, cols])
    for move, span in zip(moves, spans):
        move.wait()
        for cols in columns_of(out_ref.shape[1]):
            out_ref[:, cols] += matmul(facing_ref[:, span], other_ref[span, cols])
    for move in moves[len(spans) :]:
        move.wait()
    out_ref[...] += extra_ref[...]


def opening(unit, rates, facing, own, w_rec, extra, state, leak):
    return pl.pallas_call(
        opening_kernel,
        out_shape=(
            pltpu.VMEM(own.shape, BF16),
            pltpu.VMEM(extra.shape, F32),
            pltpu.VMEM(state.shape, F32),
            pltpu.VMEM(leak.shape, F32),
            pltpu.VMEM(extra.shape, F32),
        ),
        in_specs=[SM] + [VM] * 3 + [HB] * 4,
        out_specs=(VM,) * 5,
        scratch_shapes=[pltpu.SemaphoreType.DMA((5,))],
        compiler_params=params(),
        name="opening",
    )(unit, rates, facing, own, *[far(array) for array in (w_rec, extra, state, leak)])


def stacked(refs):
    return jnp.concatenate([ref[...] for ref in refs], axis=0)


def pick_half_kernel(*refs):
    rates, (select_ref, out_ref) = refs[:-2], refs[-2:]
    out_ref[...] = matmul(stacked(rates), select_ref[...])


def pick_half(rates, select):
    return pl.pallas_call(
        pick_half_kernel,
        out_shape=shaped((len(rates) * rates[0].shape[0], select.shape[1]), F32),
        in_specs=[VM] * (len(rates) + 1),
        out_specs=VM,
        compiler_params=params(),
        name="pick_half",
    )(*rates, select)


def pick_kernel(*refs):
    rates, (half_ref, select_ref, out_ref) = refs[:-3], refs[-3:]
    picked = half_ref[...] + matmul(stacked(rates), select_ref[...])
    out_ref[...] = picked.astype(BF16).reshape(out_ref.shape)


def pick(rates, half, select):
    return pl.pallas_call(
        pick_kernel,
        out_shape=shaped((len(rates), rates[0].shape[0], select.shape[1]), BF16),
        in_specs=[VM] * (len(rates) + 2),
        out_specs=VM,
        compiler_params=params(),
        name="pick",
    )(*rates, half, select)


def half_kernel(drive_ref, weight_ref, out_ref):
    for cols in columns_of(out_ref.shape[1]):
        out_ref[:, cols] = matmul(drive_ref[...], weight_ref[:, cols])


def half_current(drive, weight):
    return pl.pallas_call(
        half_kernel,
        out_shape=shaped((drive.shape[0], weight.shape[1]), F32),
        in_specs=[VM, VM],
        out_specs=VM,
        compiler_params=params(),
        name="half",
    )(drive, weight)


def own_kernel(rates_ref, weight_ref, extra_ref, out_ref):
    for cols in columns_of(out_ref.shape[1]):
        out_ref[:, cols] = extra_ref[:, cols] + matmul(rates_ref[...], weight_ref[:, cols])


def own_part(rates, weight, extra):
    return pl.pallas_call(
        own_kernel,
        out_shape=shaped(extra.shape, F32),
        in_specs=[VM] * 3,
        out_specs=VM,
        compiler_params=params(),
        name="own_part",
    )(rates, weight, extra)


def renewed(cols, total, state_ref, leak_ref):
    state = state_ref[:, cols]
    return state + leak_ref[:, cols] * (total - state)


def step_kernel(flow, drives, last, sum_ref, state_ref, leak_ref, *refs):
    refs = list(refs)
    rates_ref, weight_ref = (refs.pop(0), refs.pop(0)) if flow else (None, None)
    if drives:
        half_ref, drive_ref, in_ref = (refs.pop(0) for _ in range(3))
    else:
        kept_ref = refs.pop(0)
    trials = state_ref.shape[0]
    moves = []

    def send(source, target):
        moves.append(pltpu.make_async_copy(source, target, sems.at[len(moves)]))
        moves[-1].start()

    if last:
        sems, state_buf, fresh, new_ref, all_ref = (refs.pop(index) for index in (-1, -1, -1, -2, -1))
        pick_own_ref, pick_other_ref, first_ref, second_ref = (refs.pop(0) for _ in range(4))
        count = len(refs) // 2
        old = 0
        for ref in (first_ref, second_ref):
            send(ref, all_ref.at[pl.ds(old, ref.shape[0])])
            old += ref.shape[0]
        picked = matmul(stacked(refs[:count]), pick_own_ref[...])
        picked += matmul(stacked(refs[count:]), pick_other_ref[...])
        fresh[...] = picked.astype(BF16).reshape(fresh.shape)
        send(fresh, all_ref.at[pl.ds(old, fresh.shape[0])])
    else:
        state_buf, next_ref = refs[:2]
    for cols in columns_of(state_buf.shape[1]):
        total = sum_ref[:, cols]
        if flow:
            total += matmul(rates_ref[...], weight_ref[:, cols])
        if drives:
            current = half_ref[:, cols] + matmul(drive_ref[...], in_ref[:, cols])
            refs[2][:, cols] = current[trials:, :]
            total += current[:trials, :]
        else:
            total += kept_ref[:, cols]
        state = renewed(cols, total, state_ref, leak_ref)
        state_buf[:, cols] = state
        if last:
            send(state_buf.at[:, cols], new_ref.at[:, cols])
        else:
            next_ref[:, cols] = jnp.tanh(state).astype(BF16)
    for move in moves:
        move.wait()


def step(total, state, leak, flow, drives, kept):
    outs = [shaped(state.shape, F32), shaped(state.shape, BF16)]
    given = list(flow or ())
    if drives:
        given += drives
        outs.append(shaped(state.shape, F32))
    else:
        given.append(kept)
    return pl.pallas_call(
        functools.partial(step_kernel, flow is not None, drives is not None, False),
        out_shape=tuple(outs),
        in_specs=[VM] * (3 + len(given)),
        out_specs=(VM,) * len(outs),
        compiler_params=params(),
        name="step",
    )(total, state, leak, *given)


def last_step(total, state, leak, flow, kept, selects, old, pairs):
    owns, others = zip(*pairs)
    trials, part = old[0].shape[1:]
    first = sum(value.shape[0] for value in old)
    given = [*flow, kept, *selects, *old, *owns, *others]
    return pl.pallas_call(
        functools.partial(step_kernel, True, False, True),
        out_shape=(shaped(state.shape, F32), shaped((first + len(pairs), trials, part), BF16)),
        in_specs=[VM] * (3 + len(given)),
        out_specs=(HB, HB),
        scratch_shapes=[
            pltpu.VMEM((len(pairs), trials, part), BF16),
            pltpu.VMEM(state.shape, F32),
            pltpu.SemaphoreType.DMA((len(old) + 1 + len(columns_of(state.shape[1])),)),
        ],
        compiler_params=params(),
        name="last_step",
    )(total, state, leak, *given)


def coded(value):
    return jnp.round(value * CODE).astype(jnp.int32).astype(jnp.int16)


def decoded(value):
    return value.astype(jnp.int32).astype(F32) * (1.0 / CODE)


def partial_kernel(times, lines, slots, coef_ref, *refs):
    fields, outs = refs[: len(slots)], refs[len(slots) :]
    trials = fields[0].shape[-2]
    size = 16 if trials % 16 == 0 else trials
    spans = {}
    for ref, (who, first) in zip(fields, slots):
        for pos in range(ref.shape[0]):
            spans[who, first + pos] = (ref, pos)
    for start in range(0, trials, size):
        band = slice(start, start + size)
        for index, time in enumerate(times):
            totals = [None] * lines
            for who in range(2):
                for lag in LAGS:
                    ref, pos = spans[who, time - lag]
                    value = ref[pos, band, :].astype(F32)
                    for line in range(lines):
                        row = (line * 2 + who) * len(LAGS) + lag - WIN
                        term = coef_ref[row : row + 1, :] * value
                        totals[line] = term if totals[line] is None else totals[line] + term
            for line in range(lines):
                outs[line][index, band, :] = totals[line] if line == 0 else coded(totals[line])


def partials(coef, times, lines, fields):
    shape = (len(times),) + fields[0][2].shape[1:]
    outs = [shaped(shape, F32)] + [shaped(shape, jnp.int16)] * (lines - 1)
    return pl.pallas_call(
        functools.partial(partial_kernel, times, lines, [field[:2] for field in fields]),
        out_shape=tuple(outs),
        in_specs=[VM] * (1 + len(fields)),
        out_specs=(VM,) * len(outs),
        compiler_params=params(),
        name="partials",
    )(coef, *[field[2] for field in fields])


def drive_kernel(own_ref, *refs):
    total = own_ref[...]
    for ref in refs[:-1]:
        total += decoded(ref[...])
    refs[-1][...] = total.astype(BF16).reshape(refs[-1].shape)


def drive_of(own, arrived):
    span, trials, part = own.shape
    return pl.pallas_call(
        drive_kernel,
        out_shape=shaped((span * trials, part), BF16),
        in_specs=[VM] * (1 + len(arrived)),
        out_specs=VM,
        compiler_params=params(),
        name="drive",
    )(own, *arrived)


def body(*args):
    return narrow_body(*args)


def narrow_body(state_start, history, external, leak, w_rec, w_in, sources, delays, gains, proj_units):
    area = lax.axis_index("area").astype(jnp.int32).reshape(1)
    unit = lax.axis_index("unit").astype(jnp.int32).reshape(1)
    lines = lax.axis_size("area") // 2
    leak_row = leak.reshape(1, -1)

    facing = crossed(history, "area", 1)
    rates = jnp.tanh(state_start).astype(BF16)
    other = crossed(rates, "unit", 1)
    history, rec_own, in_own, in_other, select_own, select_other, coef = stage(
        area, unit, (sources, delays, gains), proj_units, history, w_rec, w_in, lines
    )
    selects = (select_own, select_other)
    known = [(0, -2 * WIN, history), (1, -2 * WIN, facing)]

    def send(times):
        sums = partials(coef, times, lines, known)
        arrived = []
        for line in range(1, lines):
            arrived.append(crossed(sums[line], "area", 2 * line))
        return sums[0], arrived

    def drive_pair(group):
        own = drive_of(*group)
        met = crossed(own, "unit", 1)
        return [half_current(own, in_own), met, in_other]

    def share(value, first):
        return [(0, first, value), (1, first, crossed(value, "area", 1))]

    half = pick_half([rates], select_own)
    fresh = pick([other], half, select_other)
    sent = send((0, 1))
    known += share(fresh, 0)
    rec_other, external, state, leak_row, total = opening(
        unit, rates, other, rec_own, w_rec, external, state_start, leak_row
    )
    old, pairs, flow, kept = [fresh], [], None, None
    for time in range(STEPS):
        if time > 0:
            other = crossed(rates, "unit", 1)
            pairs.append((rates, other))
            flow = (other, rec_other)
            if time == 2:
                owns, others = zip(*pairs)
                half = pick_half(owns, select_own)
                fresh = pick(others, half, select_other)
                old.append(fresh)
                pairs = []
                known += share(fresh, 1)
            total = own_part(rates, rec_own, external)
        if time == STEPS - 1:
            return last_step(total, state, leak_row, flow, kept, selects, old, pairs)
        drives = drive_pair(sent) if time % 2 == 0 else None
        if time in (0, 2):
            sent = send((time + 2, time + 3))
        state, rates, *more = step(total, state, leak_row, flow, drives, kept)
        kept = more[0] if more else None


def wide_body(state_start, history, external, leak, w_rec, w_in, sources, delays, gains, proj_units):
    area_count = lax.axis_size("area")
    area_index = lax.axis_index("area")
    area_total = sources.shape[0]
    share = area_count // area_total
    own_area = area_index // share
    own_src = lax.dynamic_slice_in_dim(sources, own_area, 1, 0)[0]
    own_delay = lax.dynamic_slice_in_dim(delays, own_area, 1, 0)[0]
    own_gain = lax.dynamic_slice_in_dim(gains, own_area, 1, 0)[0]
    own_valid = own_src >= 0
    trial_count = state_start.shape[0]
    proj_part = proj_units.shape[0]
    unit_full = w_rec.shape[0]
    proj_full = w_in.shape[0]
    bit_count = share.bit_length() - 1
    select = (jnp.arange(unit_full, dtype=jnp.int32)[:, None] == proj_units[None, :]).astype(BF16)
    state_now = state_start
    received = []
    outgoing = history
    produced = []
    for window_idx in range(WINDOWS):
        move_span_len = outgoing.shape[0]
        flat = outgoing.reshape(1, -1)
        wanted = (own_src[:, None] * share + jnp.arange(share, dtype=jnp.int32)[None, :]).reshape(-1)
        piece = lax.all_gather(flat, "area", axis=0, tiled=True)
        count = piece.shape[0]
        match = wanted[:, None] == jnp.arange(count, dtype=jnp.int32)[None, :]
        total = jnp.dot(match.astype(BF16), piece, preferred_element_type=F32)
        received.append(
            total.astype(BF16).reshape(MAXSRC, share, move_span_len, trial_count, proj_part)
        )
        known = jnp.concatenate(received, axis=2)
        span_len = known.shape[2]
        times = window_idx * WIN + jnp.arange(WIN, dtype=jnp.int32)
        target_idx = times[:, None] - own_delay[None, :] + 2 * WIN
        columns = jnp.arange(span_len, dtype=jnp.int32)
        chosen_steps = (columns[None, None, :] == target_idx[:, :, None]) & own_valid[None, :, None]
        weight = jnp.where(chosen_steps, own_gain[None, :, None], jnp.float32(0.0))
        summed = jnp.einsum(
            "ikj,kqjbp->ibqp", weight, known.astype(F32), precision=lax.Precision.HIGHEST
        )
        drive_part = summed.astype(BF16)
        drive_full = lax.all_gather(drive_part[:, :, :, None, :], "unit", axis=3, tiled=True)
        current = jnp.dot(
            drive_full.reshape(WIN * trial_count, proj_full), w_in, preferred_element_type=F32
        )
        current = current.reshape(WIN, trial_count, -1)
        fresh = []
        for inner_step in range(WIN):
            rate_rows = jnp.tanh(state_now).astype(BF16)
            joined = lax.all_gather(rate_rows, "unit", axis=1, tiled=True)
            for bit in range(bit_count):
                other = swapped(joined, "area", bit)
                upper = area_index // (1 << bit) % 2 == 1
                joined = jnp.where(
                    upper,
                    jnp.concatenate([other, joined], axis=1),
                    jnp.concatenate([joined, other], axis=1),
                )
            recur = jnp.dot(joined, w_rec, preferred_element_type=F32)
            picked = jnp.dot(joined, select, preferred_element_type=F32)
            fresh.append(picked.astype(BF16))
            state_now = state_now + leak[None, :] * (
                -state_now + recur + current[inner_step] + external
            )
        outgoing = jnp.stack(fresh)
        produced.append(outgoing)
    return (state_now, jnp.concatenate(produced, axis=0))


def solution(mesh):
    split = P(None, ("groups", "area", "unit"))
    placed = (
        split,
        P(None, None, ("groups", "area", "unit")),
        split,
        P(("groups", "area", "unit")),
        split,
        split,
        P("groups", None),
        P("groups", None),
        P("groups", None),
        P(("groups", "area", "unit")),
    )

    def chosen(*args):
        areas = lax.axis_size("area")
        narrow = args[6].shape[0] == areas and lax.axis_size("unit") == 2 and areas & (areas - 1) == 0
        return (body if narrow else wide_body)(*args)

    return jax.shard_map(
        chosen,
        mesh=mesh,
        in_specs=placed,
        out_specs=(split, P(None, None, ("groups", "area", "unit"))),
        check_vma=False,
    )
```

```python
import functools

import jax
import jax.numpy as jnp
from jax import lax
from jax.experimental import pallas as pl
from jax.experimental.pallas import tpu as pltpu
from jax.sharding import PartitionSpec as P

MAXSRC = 6
WIN = 3
WINDOWS = 2
STEPS = WIN * WINDOWS
BF16 = jnp.bfloat16
F32 = jnp.float32
VM = pl.BlockSpec(memory_space=pltpu.VMEM)
SM = pl.BlockSpec(memory_space=pltpu.SMEM)
HB = pl.BlockSpec(memory_space=pltpu.MemorySpace.HBM)
LAGS = range(WIN, 2 * WIN + 1)
MIB = 1 << 20
CODE = 8192.0


def swapped(value, axis, stride):
    mask = 2**stride
    return crossed(value, axis, mask)


def crossed(value, axis, mask):
    pairs = [(source, source ^ mask) for source in range(lax.axis_size(axis))]
    return lax.ppermute(value, axis, pairs)


def shaped(shape, kind):
    return jax.ShapeDtypeStruct(shape, kind)


def params(limit=8):
    return pltpu.CompilerParams(vmem_limit_bytes=limit * MIB)


def columns_of(width):
    size = 256 if width % 256 == 0 else width
    return [slice(start, start + size) for start in range(0, width, size)]


def matmul(left, right):
    return jnp.dot(left, right, preferred_element_type=F32)


def far(array):
    return pltpu.with_memory_space_constraint(array, pltpu.MemorySpace.HBM)


def half_of(unit, count):
    return pl.ds(pl.multiple_of(unit * count, count), count)


def started(moves, sems):
    found = []
    for index, (source, target) in enumerate(moves):
        found.append(pltpu.make_async_copy(source, target, sems.at[index]))
        found[-1].start()
    return found


def stage_kernel(
    lines,
    area_ref,
    unit_ref,
    src_ref,
    delay_ref,
    gain_ref,
    units_ref,
    history_far,
    rec_far,
    in_far,
    history_ref,
    rec_ref,
    in_own_ref,
    in_other_ref,
    own_ref,
    other_ref,
    coef_ref,
    sems,
):
    area, unit = area_ref[0], unit_ref[0]
    count = rec_ref.shape[0]
    part = in_own_ref.shape[0]
    moves = started(
        [
            (history_far, history_ref),
            (rec_far.at[half_of(unit, count), :], rec_ref),
            (in_far.at[half_of(unit, part), :], in_own_ref),
            (in_far.at[half_of(1 - unit, part), :], in_other_ref),
        ],
        sems,
    )
    width = coef_ref.shape[1]
    row = 0
    for line in range(lines):
        target = area ^ (2 * line)
        for who in range(2):
            source = area ^ who
            delay, gain = jnp.int32(0), jnp.float32(0.0)
            for slot in range(MAXSRC):
                match = src_ref[target, slot] == source
                delay += jnp.where(match, delay_ref[target, slot], 0)
                gain += jnp.where(match, gain_ref[target, slot], 0.0)
            for lag in LAGS:
                value = jnp.where(delay == lag, gain, 0.0)
                coef_ref[row : row + 1, :] = jnp.full((1, width), value, F32)
                row += 1
    units = units_ref[...].reshape(1, width)
    for half, ref in ((unit, own_ref), (1 - unit, other_ref)):
        block = 256 if count % 256 == 0 else count
        for start in range(0, count, block):
            ids = lax.broadcasted_iota(jnp.int32, (block, width), 0) + (start + half * count)
            ref[start : start + block, :] = jnp.where(ids == units, 1.0, 0.0).astype(BF16)
    for move in moves:
        move.wait()


def stage(area, unit, tables, units, history, w_rec, w_in, lines):
    part = units.shape[0]
    count = w_rec.shape[0] // 2
    return pl.pallas_call(
        functools.partial(stage_kernel, lines),
        out_shape=(
            pltpu.VMEM(history.shape, BF16),
            pltpu.VMEM((count, w_rec.shape[1]), BF16),
            pltpu.VMEM((w_in.shape[0] // 2, w_in.shape[1]), BF16),
            pltpu.VMEM((w_in.shape[0] // 2, w_in.shape[1]), BF16),
            pltpu.VMEM((count, part), BF16),
            pltpu.VMEM((count, part), BF16),
            pltpu.VMEM((lines * 2 * len(LAGS), part), F32),
        ),
        in_specs=[SM] * 5 + [VM] + [HB] * 3,
        out_specs=(VM,) * 7,
        scratch_shapes=[pltpu.SemaphoreType.DMA((4,))],
        compiler_params=params(),
        name="stage",
    )(area, unit, *[far(table) for table in tables], far(units), far(history), far(w_rec), far(w_in))


def opening_kernel(
    unit_ref,
    rates_ref,
    facing_ref,
    own_ref,
    rec_far,
    extra_far,
    state_far,
    leak_far,
    other_ref,
    extra_ref,
    state_ref,
    leak_ref,
    out_ref,
    sems,
):
    unit = unit_ref[0]
    count = other_ref.shape[0]
    size = count // 2 if count % 512 == 0 else count
    spans = [slice(start, start + size) for start in range(0, count, size)]
    moves = [
        (rec_far.at[pl.ds(pl.multiple_of((1 - unit) * count + span.start, size), size), :], other_ref.at[span, :])
        for span in spans
    ]
    moves += [
        (extra_far, extra_ref),
        (state_far, state_ref),
        (leak_far, leak_ref),
    ]
    moves = started(moves, sems)
    for cols in columns_of(out_ref.shape[1]):
        out_ref[:, cols] = matmul(rates_ref[...], own_ref[:, cols])
    for move, span in zip(moves, spans):
        move.wait()
        for cols in columns_of(out_ref.shape[1]):
            out_ref[:, cols] += matmul(facing_ref[:, span], other_ref[span, cols])
    for move in moves[len(spans) :]:
        move.wait()
    out_ref[...] += extra_ref[...]


def opening(unit, rates, facing, own, w_rec, extra, state, leak):
    return pl.pallas_call(
        opening_kernel,
        out_shape=(
            pltpu.VMEM(own.shape, BF16),
            pltpu.VMEM(extra.shape, F32),
            pltpu.VMEM(state.shape, F32),
            pltpu.VMEM(leak.shape, F32),
            pltpu.VMEM(extra.shape, F32),
        ),
        in_specs=[SM] + [VM] * 3 + [HB] * 4,
        out_specs=(VM,) * 5,
        scratch_shapes=[pltpu.SemaphoreType.DMA((5,))],
        compiler_params=params(),
        name="opening",
    )(unit, rates, facing, own, *[far(array) for array in (w_rec, extra, state, leak)])


def stacked(refs):
    return jnp.concatenate([ref[...] for ref in refs], axis=0)


def pick_half_kernel(*refs):
    rates, (select_ref, out_ref) = refs[:-2], refs[-2:]
    out_ref[...] = matmul(stacked(rates), select_ref[...])


def pick_half(rates, select):
    return pl.pallas_call(
        pick_half_kernel,
        out_shape=shaped((len(rates) * rates[0].shape[0], select.shape[1]), F32),
        in_specs=[VM] * (len(rates) + 1),
        out_specs=VM,
        compiler_params=params(),
        name="pick_half",
    )(*rates, select)


def pick_kernel(*refs):
    rates, (half_ref, select_ref, out_ref) = refs[:-3], refs[-3:]
    picked = half_ref[...] + matmul(stacked(rates), select_ref[...])
    out_ref[...] = picked.astype(BF16).reshape(out_ref.shape)


def pick(rates, half, select):
    return pl.pallas_call(
        pick_kernel,
        out_shape=shaped((len(rates), rates[0].shape[0], select.shape[1]), BF16),
        in_specs=[VM] * (len(rates) + 2),
        out_specs=VM,
        compiler_params=params(),
        name="pick",
    )(*rates, half, select)


def half_kernel(drive_ref, weight_ref, out_ref):
    for cols in columns_of(out_ref.shape[1]):
        out_ref[:, cols] = matmul(drive_ref[...], weight_ref[:, cols])


def half_current(drive, weight):
    return pl.pallas_call(
        half_kernel,
        out_shape=shaped((drive.shape[0], weight.shape[1]), F32),
        in_specs=[VM, VM],
        out_specs=VM,
        compiler_params=params(),
        name="half",
    )(drive, weight)


def full_kernel(half_ref, drive_ref, weight_ref, out_ref):
    for cols in columns_of(out_ref.shape[1]):
        out_ref[:, cols] = half_ref[:, cols] + matmul(drive_ref[...], weight_ref[:, cols])


def full_current(half, drive, weight):
    return pl.pallas_call(
        full_kernel,
        out_shape=shaped(half.shape, F32),
        in_specs=[VM] * 3,
        out_specs=VM,
        compiler_params=params(),
        name="full",
    )(half, drive, weight)


def own_kernel(rates_ref, weight_ref, extra_ref, out_ref):
    for cols in columns_of(out_ref.shape[1]):
        out_ref[:, cols] = extra_ref[:, cols] + matmul(rates_ref[...], weight_ref[:, cols])


def own_part(rates, weight, extra):
    return pl.pallas_call(
        own_kernel,
        out_shape=shaped(extra.shape, F32),
        in_specs=[VM] * 3,
        out_specs=VM,
        compiler_params=params(),
        name="own_part",
    )(rates, weight, extra)


def renewed(cols, total, state_ref, leak_ref):
    state = state_ref[:, cols]
    return state + leak_ref[:, cols] * (total - state)


def step_kernel(flow, drives, row, last, sum_ref, state_ref, leak_ref, *refs):
    refs = list(refs)
    rates_ref, weight_ref = (refs.pop(0), refs.pop(0)) if flow else (None, None)
    if drives:
        half_ref, drive_ref, in_ref = (refs.pop(0) for _ in range(3))
    else:
        kept_ref = refs.pop(0)
    trials = state_ref.shape[0]
    moves = []

    def send(source, target):
        moves.append(pltpu.make_async_copy(source, target, sems.at[len(moves)]))
        moves[-1].start()

    if last:
        sems, state_buf, fresh, new_ref, all_ref = (refs.pop(index) for index in (-1, -1, -1, -2, -1))
        pick_own_ref, pick_other_ref, first_ref, second_ref = (refs.pop(0) for _ in range(4))
        count = len(refs) // 2
        old = 0
        for ref in (first_ref, second_ref):
            send(ref, all_ref.at[pl.ds(old, ref.shape[0])])
            old += ref.shape[0]
        picked = matmul(stacked(refs[:count]), pick_own_ref[...])
        picked += matmul(stacked(refs[count:]), pick_other_ref[...])
        fresh[...] = picked.astype(BF16).reshape(fresh.shape)
        send(fresh, all_ref.at[pl.ds(old, fresh.shape[0])])
    else:
        state_buf, next_ref = refs[:2]
    for cols in columns_of(state_buf.shape[1]):
        total = sum_ref[:, cols]
        if flow:
            total += matmul(rates_ref[...], weight_ref[:, cols])
        if drives:
            current = half_ref[:, cols] + matmul(drive_ref[...], in_ref[:, cols])
            refs[2][:, cols] = current[trials:, :]
            total += current[:trials, :]
        else:
            total += kept_ref[row * trials : (row + 1) * trials, cols]
        state = renewed(cols, total, state_ref, leak_ref)
        state_buf[:, cols] = state
        if last:
            send(state_buf.at[:, cols], new_ref.at[:, cols])
        else:
            next_ref[:, cols] = jnp.tanh(state).astype(BF16)
    for move in moves:
        move.wait()


def step(total, state, leak, flow, drives, kept, row):
    outs = [shaped(state.shape, F32), shaped(state.shape, BF16)]
    given = list(flow or ())
    if drives:
        given += drives
        outs.append(shaped(state.shape, F32))
    else:
        given.append(kept)
    return pl.pallas_call(
        functools.partial(step_kernel, flow is not None, drives is not None, row, False),
        out_shape=tuple(outs),
        in_specs=[VM] * (3 + len(given)),
        out_specs=(VM,) * len(outs),
        compiler_params=params(),
        name="step",
    )(total, state, leak, *given)


def last_step(total, state, leak, flow, kept, selects, old, pairs):
    owns, others = zip(*pairs)
    trials, part = old[0].shape[1:]
    first = sum(value.shape[0] for value in old)
    given = [*flow, kept, *selects, *old, *owns, *others]
    return pl.pallas_call(
        functools.partial(step_kernel, True, False, 0, True),
        out_shape=(shaped(state.shape, F32), shaped((first + len(pairs), trials, part), BF16)),
        in_specs=[VM] * (3 + len(given)),
        out_specs=(HB, HB),
        scratch_shapes=[
            pltpu.VMEM((len(pairs), trials, part), BF16),
            pltpu.VMEM(state.shape, F32),
            pltpu.SemaphoreType.DMA((len(old) + 1 + len(columns_of(state.shape[1])),)),
        ],
        compiler_params=params(),
        name="last_step",
    )(total, state, leak, *given)


def coded(value):
    return jnp.round(value * CODE).astype(jnp.int32).astype(jnp.int16)


def decoded(value):
    return value.astype(jnp.int32).astype(F32) * (1.0 / CODE)


def partial_kernel(times, lines, slots, base, final, coef_ref, *refs):
    bases, refs = refs[:base], refs[base:]
    fields, outs = refs[: len(slots)], refs[len(slots) :]
    trials = fields[0].shape[-2]
    size = 16 if trials % 16 == 0 else trials
    spans = {}
    for ref, (who, first) in zip(fields, slots):
        for pos in range(ref.shape[0]):
            spans[who, first + pos] = (ref, pos)
    for start in range(0, trials, size):
        band = slice(start, start + size)
        for index, time in enumerate(times):
            totals = [ref[index, band, :] for ref in bases] or [None] * lines
            for who in range(2):
                for lag in LAGS:
                    if (who, time - lag) not in spans:
                        continue
                    ref, pos = spans[who, time - lag]
                    value = ref[pos, band, :].astype(F32)
                    for line in range(lines):
                        row = (line * 2 + who) * len(LAGS) + lag - WIN
                        term = coef_ref[row : row + 1, :] * value
                        totals[line] = term if totals[line] is None else totals[line] + term
            for line in range(lines):
                sent = final and line > 0
                outs[line][index, band, :] = coded(totals[line]) if sent else totals[line]


def partials(coef, times, lines, fields, bases=(), final=True):
    shape = (len(times),) + fields[0][2].shape[1:]
    outs = [shaped(shape, F32)] + [shaped(shape, jnp.int16 if final else F32)] * (lines - 1)
    return pl.pallas_call(
        functools.partial(
            partial_kernel, times, lines, [field[:2] for field in fields], len(bases), final
        ),
        out_shape=tuple(outs),
        in_specs=[VM] * (1 + len(bases) + len(fields)),
        out_specs=(VM,) * len(outs),
        compiler_params=params(),
        name="partials",
    )(coef, *bases, *[field[2] for field in fields])


def drive_kernel(own_ref, *refs):
    total = own_ref[...]
    for ref in refs[:-1]:
        total += decoded(ref[...])
    refs[-1][...] = total.astype(BF16).reshape(refs[-1].shape)


def drive_of(own, arrived):
    span, trials, part = own.shape
    return pl.pallas_call(
        drive_kernel,
        out_shape=shaped((span * trials, part), BF16),
        in_specs=[VM] * (1 + len(arrived)),
        out_specs=VM,
        compiler_params=params(),
        name="drive",
    )(own, *arrived)


def body(*args):
    return narrow_body(*args)


def narrow_body(state_start, history, external, leak, w_rec, w_in, sources, delays, gains, proj_units):
    area = lax.axis_index("area").astype(jnp.int32).reshape(1)
    unit = lax.axis_index("unit").astype(jnp.int32).reshape(1)
    lines = lax.axis_size("area") // 2
    leak_row = leak.reshape(1, -1)

    facing = crossed(history, "area", 1)
    rates = jnp.tanh(state_start).astype(BF16)
    other = crossed(rates, "unit", 1)
    history, rec_own, in_own, in_other, select_own, select_other, coef = stage(
        area, unit, (sources, delays, gains), proj_units, history, w_rec, w_in, lines
    )
    selects = (select_own, select_other)
    known = [(0, -2 * WIN, history), (1, -2 * WIN, facing)]

    def send(times, ready, late):
        if late:
            bases = partials(coef, times, lines, ready, final=False)
            sums = partials(coef, times, lines, late, bases)
        else:
            sums = partials(coef, times, lines, ready)
        arrived = []
        for line in range(1, lines):
            arrived.append(crossed(sums[line], "area", 2 * line))
        return sums[0], arrived

    def drive_pair(group):
        own = drive_of(*group)
        met = crossed(own, "unit", 1)
        return [half_current(own, in_own), met, in_other]

    def share(value, first):
        return [(0, first, value), (1, first, crossed(value, "area", 1))]

    half = pick_half([rates], select_own)
    fresh = pick([other], half, select_other)
    sent = send((0, 1), known, None)
    known += share(fresh, 0)
    rec_other, external, state, leak_row, total = opening(
        unit, rates, other, rec_own, w_rec, external, state_start, leak_row
    )
    old, pairs, flow, kept = [fresh], [], None, None
    for time in range(STEPS):
        if time > 0:
            other = crossed(rates, "unit", 1)
            pairs.append((rates, other))
            flow = (other, rec_other)
            if time == 2:
                owns, others = zip(*pairs)
                half = pick_half(owns, select_own)
                fresh = pick(others, half, select_other)
                old.append(fresh)
                pairs = []
                here, there = share(fresh, 1)
            total = own_part(rates, rec_own, external)
        if time == STEPS - 1:
            return last_step(total, state, leak_row, flow, kept, selects, old, pairs)
        drives, row = drive_pair(sent) if time % 2 == 0 else None, 0
        if time == 2:
            kept, drives = full_current(*drives), None
            sent = send((4, 5), known + [here], [there])
        if time == 3:
            row = 1
        if time == 0:
            sent = send((2, 3), known, None)
        state, rates, *more = step(total, state, leak_row, flow, drives, kept, row)
        kept = more[0] if more else kept


def wide_body(state_start, history, external, leak, w_rec, w_in, sources, delays, gains, proj_units):
    area_count = lax.axis_size("area")
    area_index = lax.axis_index("area")
    area_total = sources.shape[0]
    share = area_count // area_total
    own_area = area_index // share
    own_src = lax.dynamic_slice_in_dim(sources, own_area, 1, 0)[0]
    own_delay = lax.dynamic_slice_in_dim(delays, own_area, 1, 0)[0]
    own_gain = lax.dynamic_slice_in_dim(gains, own_area, 1, 0)[0]
    own_valid = own_src >= 0
    trial_count = state_start.shape[0]
    proj_part = proj_units.shape[0]
    unit_full = w_rec.shape[0]
    proj_full = w_in.shape[0]
    bit_count = share.bit_length() - 1
    select = (jnp.arange(unit_full, dtype=jnp.int32)[:, None] == proj_units[None, :]).astype(BF16)
    state_now = state_start
    received = []
    outgoing = history
    produced = []
    for window_idx in range(WINDOWS):
        move_span_len = outgoing.shape[0]
        flat = outgoing.reshape(1, -1)
        wanted = (own_src[:, None] * share + jnp.arange(share, dtype=jnp.int32)[None, :]).reshape(-1)
        piece = lax.all_gather(flat, "area", axis=0, tiled=True)
        count = piece.shape[0]
        match = wanted[:, None] == jnp.arange(count, dtype=jnp.int32)[None, :]
        total = jnp.dot(match.astype(BF16), piece, preferred_element_type=F32)
        received.append(
            total.astype(BF16).reshape(MAXSRC, share, move_span_len, trial_count, proj_part)
        )
        known = jnp.concatenate(received, axis=2)
        span_len = known.shape[2]
        times = window_idx * WIN + jnp.arange(WIN, dtype=jnp.int32)
        target_idx = times[:, None] - own_delay[None, :] + 2 * WIN
        columns = jnp.arange(span_len, dtype=jnp.int32)
        chosen_steps = (columns[None, None, :] == target_idx[:, :, None]) & own_valid[None, :, None]
        weight = jnp.where(chosen_steps, own_gain[None, :, None], jnp.float32(0.0))
        summed = jnp.einsum(
            "ikj,kqjbp->ibqp", weight, known.astype(F32), precision=lax.Precision.HIGHEST
        )
        drive_part = summed.astype(BF16)
        drive_full = lax.all_gather(drive_part[:, :, :, None, :], "unit", axis=3, tiled=True)
        current = jnp.dot(
            drive_full.reshape(WIN * trial_count, proj_full), w_in, preferred_element_type=F32
        )
        current = current.reshape(WIN, trial_count, -1)
        fresh = []
        for inner_step in range(WIN):
            rate_rows = jnp.tanh(state_now).astype(BF16)
            joined = lax.all_gather(rate_rows, "unit", axis=1, tiled=True)
            for bit in range(bit_count):
                other = swapped(joined, "area", bit)
                upper = area_index // (1 << bit) % 2 == 1
                joined = jnp.where(
                    upper,
                    jnp.concatenate([other, joined], axis=1),
                    jnp.concatenate([joined, other], axis=1),
                )
            recur = jnp.dot(joined, w_rec, preferred_element_type=F32)
            picked = jnp.dot(joined, select, preferred_element_type=F32)
            fresh.append(picked.astype(BF16))
            state_now = state_now + leak[None, :] * (
                -state_now + recur + current[inner_step] + external
            )
        outgoing = jnp.stack(fresh)
        produced.append(outgoing)
    return (state_now, jnp.concatenate(produced, axis=0))


def solution(mesh):
    split = P(None, ("groups", "area", "unit"))
    placed = (
        split,
        P(None, None, ("groups", "area", "unit")),
        split,
        P(("groups", "area", "unit")),
        split,
        split,
        P("groups", None),
        P("groups", None),
        P("groups", None),
        P(("groups", "area", "unit")),
    )

    def chosen(*args):
        areas = lax.axis_size("area")
        narrow = args[6].shape[0] == areas and lax.axis_size("unit") == 2 and areas & (areas - 1) == 0
        return (body if narrow else wide_body)(*args)

    return jax.shard_map(
        chosen,
        mesh=mesh,
        in_specs=placed,
        out_specs=(split, P(None, None, ("groups", "area", "unit"))),
        check_vma=False,
    )
```

```python
import functools

import jax
import jax.numpy as jnp
from jax import lax
from jax.experimental import pallas as pl
from jax.experimental.pallas import tpu as pltpu
from jax.sharding import PartitionSpec as P

MAXSRC = 6
WIN = 3
WINDOWS = 2
STEPS = WIN * WINDOWS
BF16 = jnp.bfloat16
F32 = jnp.float32
VM = pl.BlockSpec(memory_space=pltpu.VMEM)
SM = pl.BlockSpec(memory_space=pltpu.SMEM)
HB = pl.BlockSpec(memory_space=pltpu.MemorySpace.HBM)
LAGS = range(WIN, 2 * WIN + 1)
MIB = 1 << 20
CODE = 8192.0


def swapped(value, axis, stride):
    mask = 2**stride
    return crossed(value, axis, mask)


def crossed(value, axis, mask):
    pairs = [(source, source ^ mask) for source in range(lax.axis_size(axis))]
    return lax.ppermute(value, axis, pairs)


def shaped(shape, kind):
    return jax.ShapeDtypeStruct(shape, kind)


def params(limit=8):
    return pltpu.CompilerParams(vmem_limit_bytes=limit * MIB)


def columns_of(width):
    size = 256 if width % 256 == 0 else width
    return [slice(start, start + size) for start in range(0, width, size)]


def matmul(left, right):
    return jnp.dot(left, right, preferred_element_type=F32)


def far(array):
    return pltpu.with_memory_space_constraint(array, pltpu.MemorySpace.HBM)


def half_of(unit, count):
    return pl.ds(pl.multiple_of(unit * count, count), count)


def started(moves, sems):
    found = []
    for index, (source, target) in enumerate(moves):
        found.append(pltpu.make_async_copy(source, target, sems.at[index]))
        found[-1].start()
    return found


def stage_kernel(
    lines,
    area_ref,
    unit_ref,
    src_ref,
    delay_ref,
    gain_ref,
    units_ref,
    history_far,
    rec_far,
    in_far,
    history_ref,
    rec_ref,
    in_own_ref,
    in_other_ref,
    own_ref,
    other_ref,
    coef_ref,
    sems,
):
    area, unit = area_ref[0], unit_ref[0]
    count = rec_ref.shape[0]
    part = in_own_ref.shape[0]
    moves = started(
        [
            (history_far, history_ref),
            (rec_far.at[half_of(unit, count), :], rec_ref),
            (in_far.at[half_of(unit, part), :], in_own_ref),
            (in_far.at[half_of(1 - unit, part), :], in_other_ref),
        ],
        sems,
    )
    width = coef_ref.shape[1]
    row = 0
    for line in range(lines):
        target = area ^ (2 * line)
        for who in range(2):
            source = area ^ who
            delay, gain = jnp.int32(0), jnp.float32(0.0)
            for slot in range(MAXSRC):
                match = src_ref[target, slot] == source
                delay += jnp.where(match, delay_ref[target, slot], 0)
                gain += jnp.where(match, gain_ref[target, slot], 0.0)
            for lag in LAGS:
                value = jnp.where(delay == lag, gain, 0.0)
                coef_ref[row : row + 1, :] = jnp.full((1, width), value, F32)
                row += 1
    units = units_ref[...].reshape(1, width)
    for half, ref in ((unit, own_ref), (1 - unit, other_ref)):
        block = 256 if count % 256 == 0 else count
        for start in range(0, count, block):
            ids = lax.broadcasted_iota(jnp.int32, (block, width), 0) + (start + half * count)
            ref[start : start + block, :] = jnp.where(ids == units, 1.0, 0.0).astype(BF16)
    for move in moves:
        move.wait()


def stage(area, unit, tables, units, history, w_rec, w_in, lines):
    part = units.shape[0]
    count = w_rec.shape[0] // 2
    return pl.pallas_call(
        functools.partial(stage_kernel, lines),
        out_shape=(
            pltpu.VMEM(history.shape, BF16),
            pltpu.VMEM((count, w_rec.shape[1]), BF16),
            pltpu.VMEM((w_in.shape[0] // 2, w_in.shape[1]), BF16),
            pltpu.VMEM((w_in.shape[0] // 2, w_in.shape[1]), BF16),
            pltpu.VMEM((count, part), BF16),
            pltpu.VMEM((count, part), BF16),
            pltpu.VMEM((lines * 2 * len(LAGS), part), F32),
        ),
        in_specs=[SM] * 5 + [VM] + [HB] * 3,
        out_specs=(VM,) * 7,
        scratch_shapes=[pltpu.SemaphoreType.DMA((4,))],
        compiler_params=params(),
        name="stage",
    )(area, unit, *[far(table) for table in tables], far(units), far(history), far(w_rec), far(w_in))


def opening_kernel(
    unit_ref,
    rates_ref,
    facing_ref,
    own_ref,
    rec_far,
    extra_far,
    state_far,
    leak_far,
    other_ref,
    extra_ref,
    state_ref,
    leak_ref,
    out_ref,
    sems,
):
    unit = unit_ref[0]
    count = other_ref.shape[0]
    size = count // 2 if count % 512 == 0 else count
    spans = [slice(start, start + size) for start in range(0, count, size)]
    moves = [
        (rec_far.at[pl.ds(pl.multiple_of((1 - unit) * count + span.start, size), size), :], other_ref.at[span, :])
        for span in spans
    ]
    moves += [
        (extra_far, extra_ref),
        (state_far, state_ref),
        (leak_far, leak_ref),
    ]
    moves = started(moves, sems)
    for cols in columns_of(out_ref.shape[1]):
        out_ref[:, cols] = matmul(rates_ref[...], own_ref[:, cols])
    for move, span in zip(moves, spans):
        move.wait()
        for cols in columns_of(out_ref.shape[1]):
            out_ref[:, cols] += matmul(facing_ref[:, span], other_ref[span, cols])
    for move in moves[len(spans) :]:
        move.wait()
    out_ref[...] += extra_ref[...]


def opening(unit, rates, facing, own, w_rec, extra, state, leak):
    return pl.pallas_call(
        opening_kernel,
        out_shape=(
            pltpu.VMEM(own.shape, BF16),
            pltpu.VMEM(extra.shape, F32),
            pltpu.VMEM(state.shape, F32),
            pltpu.VMEM(leak.shape, F32),
            pltpu.VMEM(extra.shape, F32),
        ),
        in_specs=[SM] + [VM] * 3 + [HB] * 4,
        out_specs=(VM,) * 5,
        scratch_shapes=[pltpu.SemaphoreType.DMA((5,))],
        compiler_params=params(),
        name="opening",
    )(unit, rates, facing, own, *[far(array) for array in (w_rec, extra, state, leak)])


def stacked(refs):
    return jnp.concatenate([ref[...] for ref in refs], axis=0)


def pick_half_kernel(*refs):
    rates, (select_ref, out_ref) = refs[:-2], refs[-2:]
    out_ref[...] = matmul(stacked(rates), select_ref[...])


def pick_half(rates, select):
    return pl.pallas_call(
        pick_half_kernel,
        out_shape=shaped((len(rates) * rates[0].shape[0], select.shape[1]), F32),
        in_specs=[VM] * (len(rates) + 1),
        out_specs=VM,
        compiler_params=params(),
        name="pick_half",
    )(*rates, select)


def pick_kernel(*refs):
    rates, (half_ref, select_ref, out_ref) = refs[:-3], refs[-3:]
    picked = half_ref[...] + matmul(stacked(rates), select_ref[...])
    out_ref[...] = picked.astype(BF16).reshape(out_ref.shape)


def pick(rates, half, select):
    return pl.pallas_call(
        pick_kernel,
        out_shape=shaped((len(rates), rates[0].shape[0], select.shape[1]), BF16),
        in_specs=[VM] * (len(rates) + 2),
        out_specs=VM,
        compiler_params=params(),
        name="pick",
    )(*rates, half, select)


def half_kernel(drive_ref, weight_ref, out_ref):
    for cols in columns_of(out_ref.shape[1]):
        out_ref[:, cols] = matmul(drive_ref[...], weight_ref[:, cols])


def half_current(drive, weight):
    return pl.pallas_call(
        half_kernel,
        out_shape=shaped((drive.shape[0], weight.shape[1]), F32),
        in_specs=[VM, VM],
        out_specs=VM,
        compiler_params=params(),
        name="half",
    )(drive, weight)


def full_kernel(half_ref, drive_ref, weight_ref, out_ref):
    for cols in columns_of(out_ref.shape[1]):
        out_ref[:, cols] = half_ref[:, cols] + matmul(drive_ref[...], weight_ref[:, cols])


def full_current(half, drive, weight):
    return pl.pallas_call(
        full_kernel,
        out_shape=shaped(half.shape, F32),
        in_specs=[VM] * 3,
        out_specs=VM,
        compiler_params=params(),
        name="full",
    )(half, drive, weight)


def own_kernel(rates_ref, weight_ref, extra_ref, out_ref):
    for cols in columns_of(out_ref.shape[1]):
        out_ref[:, cols] = extra_ref[:, cols] + matmul(rates_ref[...], weight_ref[:, cols])


def own_part(rates, weight, extra):
    return pl.pallas_call(
        own_kernel,
        out_shape=shaped(extra.shape, F32),
        in_specs=[VM] * 3,
        out_specs=VM,
        compiler_params=params(),
        name="own_part",
    )(rates, weight, extra)


def renewed(cols, total, state_ref, leak_ref):
    state = state_ref[:, cols]
    return state + leak_ref[:, cols] * (total - state)


def step_kernel(flow, drives, row, last, sum_ref, state_ref, leak_ref, *refs):
    refs = list(refs)
    rates_ref, weight_ref = (refs.pop(0), refs.pop(0)) if flow else (None, None)
    if drives:
        half_ref, drive_ref, in_ref = (refs.pop(0) for _ in range(3))
    else:
        kept_ref = refs.pop(0)
    trials = state_ref.shape[0]
    moves = []

    def send(source, target):
        moves.append(pltpu.make_async_copy(source, target, sems.at[len(moves)]))
        moves[-1].start()

    if last:
        sems, state_buf, fresh, new_ref, all_ref = (refs.pop(index) for index in (-1, -1, -1, -2, -1))
        pick_own_ref, pick_other_ref, *olds = (refs.pop(0) for _ in range(5))
        count = len(refs) // 2
        old = 0
        for ref in olds:
            send(ref, all_ref.at[pl.ds(old, ref.shape[0])])
            old += ref.shape[0]
        picked = matmul(stacked(refs[:count]), pick_own_ref[...])
        picked += matmul(stacked(refs[count:]), pick_other_ref[...])
        fresh[...] = picked.astype(BF16).reshape(fresh.shape)
        send(fresh, all_ref.at[pl.ds(old, fresh.shape[0])])
    else:
        state_buf, next_ref = refs[:2]
    for cols in columns_of(state_buf.shape[1]):
        total = sum_ref[:, cols]
        if flow:
            total += matmul(rates_ref[...], weight_ref[:, cols])
        if drives:
            current = half_ref[:, cols] + matmul(drive_ref[...], in_ref[:, cols])
            refs[2][:, cols] = current[trials:, :]
            total += current[:trials, :]
        else:
            total += kept_ref[row * trials : (row + 1) * trials, cols]
        state = renewed(cols, total, state_ref, leak_ref)
        state_buf[:, cols] = state
        if last:
            send(state_buf.at[:, cols], new_ref.at[:, cols])
        else:
            next_ref[:, cols] = jnp.tanh(state).astype(BF16)
    for move in moves:
        move.wait()


def step(total, state, leak, flow, drives, kept, row):
    outs = [shaped(state.shape, F32), shaped(state.shape, BF16)]
    given = list(flow or ())
    if drives:
        given += drives
        outs.append(shaped(state.shape, F32))
    else:
        given.append(kept)
    return pl.pallas_call(
        functools.partial(step_kernel, flow is not None, drives is not None, row, False),
        out_shape=tuple(outs),
        in_specs=[VM] * (3 + len(given)),
        out_specs=(VM,) * len(outs),
        compiler_params=params(),
        name="step",
    )(total, state, leak, *given)


def last_step(total, state, leak, flow, kept, selects, old, pairs):
    owns, others = zip(*pairs)
    trials, part = old[0].shape[1:]
    first = sum(value.shape[0] for value in old)
    given = [*flow, kept, *selects, *old, *owns, *others]
    return pl.pallas_call(
        functools.partial(step_kernel, True, False, 0, True),
        out_shape=(shaped(state.shape, F32), shaped((first + len(pairs), trials, part), BF16)),
        in_specs=[VM] * (3 + len(given)),
        out_specs=(HB, HB),
        scratch_shapes=[
            pltpu.VMEM((len(pairs), trials, part), BF16),
            pltpu.VMEM(state.shape, F32),
            pltpu.SemaphoreType.DMA((len(old) + 1 + len(columns_of(state.shape[1])),)),
        ],
        compiler_params=params(),
        name="last_step",
    )(total, state, leak, *given)


def coded(value):
    return jnp.round(value * CODE).astype(jnp.int32).astype(jnp.int16)


def decoded(value):
    return value.astype(jnp.int32).astype(F32) * (1.0 / CODE)


def partial_kernel(times, lines, slots, base, final, coef_ref, *refs):
    bases, refs = refs[:base], refs[base:]
    fields, outs = refs[: len(slots)], refs[len(slots) :]
    trials = fields[0].shape[-2]
    size = 16 if trials % 16 == 0 else trials
    spans = {}
    for ref, (who, first) in zip(fields, slots):
        for pos in range(ref.shape[0]):
            spans[who, first + pos] = (ref, pos)
    for start in range(0, trials, size):
        band = slice(start, start + size)
        for index, time in enumerate(times):
            totals = [ref[index, band, :] for ref in bases] or [None] * lines
            for who in range(2):
                for lag in LAGS:
                    if (who, time - lag) not in spans:
                        continue
                    ref, pos = spans[who, time - lag]
                    value = ref[pos, band, :].astype(F32)
                    for line in range(lines):
                        row = (line * 2 + who) * len(LAGS) + lag - WIN
                        term = coef_ref[row : row + 1, :] * value
                        totals[line] = term if totals[line] is None else totals[line] + term
            for line in range(lines):
                sent = final and line > 0
                outs[line][index, band, :] = coded(totals[line]) if sent else totals[line]


def partials(coef, times, lines, fields, bases=(), final=True):
    shape = (len(times),) + fields[0][2].shape[1:]
    outs = [shaped(shape, F32)] + [shaped(shape, jnp.int16 if final else F32)] * (lines - 1)
    return pl.pallas_call(
        functools.partial(
            partial_kernel, times, lines, [field[:2] for field in fields], len(bases), final
        ),
        out_shape=tuple(outs),
        in_specs=[VM] * (1 + len(bases) + len(fields)),
        out_specs=(VM,) * len(outs),
        compiler_params=params(),
        name="partials",
    )(coef, *bases, *[field[2] for field in fields])


def drive_kernel(own_ref, *refs):
    total = own_ref[...]
    for ref in refs[:-1]:
        total += decoded(ref[...])
    refs[-1][...] = total.astype(BF16).reshape(refs[-1].shape)


def drive_of(own, arrived):
    span, trials, part = own.shape
    return pl.pallas_call(
        drive_kernel,
        out_shape=shaped((span * trials, part), BF16),
        in_specs=[VM] * (1 + len(arrived)),
        out_specs=VM,
        compiler_params=params(),
        name="drive",
    )(own, *arrived)


def body(*args):
    return narrow_body(*args)


def narrow_body(state_start, history, external, leak, w_rec, w_in, sources, delays, gains, proj_units):
    area = lax.axis_index("area").astype(jnp.int32).reshape(1)
    unit = lax.axis_index("unit").astype(jnp.int32).reshape(1)
    lines = lax.axis_size("area") // 2
    leak_row = leak.reshape(1, -1)

    facing = crossed(history, "area", 1)
    rates = jnp.tanh(state_start).astype(BF16)
    other = crossed(rates, "unit", 1)
    history, rec_own, in_own, in_other, select_own, select_other, coef = stage(
        area, unit, (sources, delays, gains), proj_units, history, w_rec, w_in, lines
    )
    selects = (select_own, select_other)
    known = [(0, -2 * WIN, history), (1, -2 * WIN, facing)]

    def send(times, ready, late):
        if late:
            bases = partials(coef, times, lines, ready, final=False)
            sums = partials(coef, times, lines, late, bases)
        else:
            sums = partials(coef, times, lines, ready)
        arrived = []
        for line in range(1, lines):
            arrived.append(crossed(sums[line], "area", 2 * line))
        return sums[0], arrived

    def drive_pair(group):
        own = drive_of(*group)
        met = crossed(own, "unit", 1)
        return [half_current(own, in_own), met, in_other]

    def share(value, first):
        return [(0, first, value), (1, first, crossed(value, "area", 1))]

    half = pick_half([rates], select_own)
    fresh = pick([other], half, select_other)
    sent = send((0, 1), known, None)
    known += share(fresh, 0)
    rec_other, external, state, leak_row, total = opening(
        unit, rates, other, rec_own, w_rec, external, state_start, leak_row
    )
    old, pairs, flow, kept = [fresh], [], None, None
    for time in range(STEPS):
        if time > 0:
            other = crossed(rates, "unit", 1)
            pairs.append((rates, other))
            flow = (other, rec_other)
            if time == 2:
                owns, others = zip(*pairs)
                half = pick_half(owns, select_own)
                fresh = pick(others, half, select_other)
                old.append(fresh)
                pairs = []
                here, there = share(fresh, 1)
            total = own_part(rates, rec_own, external)
        if time == STEPS - 1:
            return last_step(total, state, leak_row, flow, kept, selects, old, pairs)
        drives, row = drive_pair(sent) if time % 2 == 0 else None, 0
        if time == 2:
            kept, drives = full_current(*drives), None
            sent = send((4, 5), known + [here], [there])
        if time == 3:
            row = 1
        if time == 0:
            sent = send((2, 3), known, None)
        if time == 4:
            owns, others = zip(*pairs)
            half = pick_half(owns, select_own)
            old.append(pick(others, half, select_other))
            pairs = []
        state, rates, *more = step(total, state, leak_row, flow, drives, kept, row)
        kept = more[0] if more else kept


def wide_body(state_start, history, external, leak, w_rec, w_in, sources, delays, gains, proj_units):
    area_count = lax.axis_size("area")
    area_index = lax.axis_index("area")
    area_total = sources.shape[0]
    share = area_count // area_total
    own_area = area_index // share
    own_src = lax.dynamic_slice_in_dim(sources, own_area, 1, 0)[0]
    own_delay = lax.dynamic_slice_in_dim(delays, own_area, 1, 0)[0]
    own_gain = lax.dynamic_slice_in_dim(gains, own_area, 1, 0)[0]
    own_valid = own_src >= 0
    trial_count = state_start.shape[0]
    proj_part = proj_units.shape[0]
    unit_full = w_rec.shape[0]
    proj_full = w_in.shape[0]
    bit_count = share.bit_length() - 1
    select = (jnp.arange(unit_full, dtype=jnp.int32)[:, None] == proj_units[None, :]).astype(BF16)
    state_now = state_start
    received = []
    outgoing = history
    produced = []
    for window_idx in range(WINDOWS):
        move_span_len = outgoing.shape[0]
        flat = outgoing.reshape(1, -1)
        wanted = (own_src[:, None] * share + jnp.arange(share, dtype=jnp.int32)[None, :]).reshape(-1)
        piece = lax.all_gather(flat, "area", axis=0, tiled=True)
        count = piece.shape[0]
        match = wanted[:, None] == jnp.arange(count, dtype=jnp.int32)[None, :]
        total = jnp.dot(match.astype(BF16), piece, preferred_element_type=F32)
        received.append(
            total.astype(BF16).reshape(MAXSRC, share, move_span_len, trial_count, proj_part)
        )
        known = jnp.concatenate(received, axis=2)
        span_len = known.shape[2]
        times = window_idx * WIN + jnp.arange(WIN, dtype=jnp.int32)
        target_idx = times[:, None] - own_delay[None, :] + 2 * WIN
        columns = jnp.arange(span_len, dtype=jnp.int32)
        chosen_steps = (columns[None, None, :] == target_idx[:, :, None]) & own_valid[None, :, None]
        weight = jnp.where(chosen_steps, own_gain[None, :, None], jnp.float32(0.0))
        summed = jnp.einsum(
            "ikj,kqjbp->ibqp", weight, known.astype(F32), precision=lax.Precision.HIGHEST
        )
        drive_part = summed.astype(BF16)
        drive_full = lax.all_gather(drive_part[:, :, :, None, :], "unit", axis=3, tiled=True)
        current = jnp.dot(
            drive_full.reshape(WIN * trial_count, proj_full), w_in, preferred_element_type=F32
        )
        current = current.reshape(WIN, trial_count, -1)
        fresh = []
        for inner_step in range(WIN):
            rate_rows = jnp.tanh(state_now).astype(BF16)
            joined = lax.all_gather(rate_rows, "unit", axis=1, tiled=True)
            for bit in range(bit_count):
                other = swapped(joined, "area", bit)
                upper = area_index // (1 << bit) % 2 == 1
                joined = jnp.where(
                    upper,
                    jnp.concatenate([other, joined], axis=1),
                    jnp.concatenate([joined, other], axis=1),
                )
            recur = jnp.dot(joined, w_rec, preferred_element_type=F32)
            picked = jnp.dot(joined, select, preferred_element_type=F32)
            fresh.append(picked.astype(BF16))
            state_now = state_now + leak[None, :] * (
                -state_now + recur + current[inner_step] + external
            )
        outgoing = jnp.stack(fresh)
        produced.append(outgoing)
    return (state_now, jnp.concatenate(produced, axis=0))


def solution(mesh):
    split = P(None, ("groups", "area", "unit"))
    placed = (
        split,
        P(None, None, ("groups", "area", "unit")),
        split,
        P(("groups", "area", "unit")),
        split,
        split,
        P("groups", None),
        P("groups", None),
        P("groups", None),
        P(("groups", "area", "unit")),
    )

    def chosen(*args):
        areas = lax.axis_size("area")
        narrow = args[6].shape[0] == areas and lax.axis_size("unit") == 2 and areas & (areas - 1) == 0
        return (body if narrow else wide_body)(*args)

    return jax.shard_map(
        chosen,
        mesh=mesh,
        in_specs=placed,
        out_specs=(split, P(None, None, ("groups", "area", "unit"))),
        check_vma=False,
    )
```
